1024 devices in a mesh: blk: 256 (over x, y, z_hi, core), rep: 4 (over z_lo).
Axes of the slice: x: 4, y: 8, z: 16 (z_hi: 4, z_lo: 4; z = z_hi * 4 + z_lo), core: 2. Of those that a mesh axis runs over, the one named last changes fastest.
Arguments:
- x_nodes: bfloat16 [131072, 512], P('blk', 'rep'), may hold values from -30 to 30
- w_qkv: bfloat16 [512, 3, 512], P(None, None, 'rep'), may hold values from -2 to 2
- w_out: bfloat16 [512, 512], P('rep'), may hold values from -0.25 to 0.25
- pair_key: int32 [2048, 8], P('blk'), may hold values from 0 to 2047, as said below
- pair_count: int32 [2048], P('blk'), may hold values from 3 to 8, as said below
- node_count: int32 [2048], replicated, may hold values from 16 to 64, as said below
Outputs:
- mixed: bfloat16 [131072, 512], P('blk', 'rep')
The draws below stay inside these ranges and needn't reach their ends.
Inputs may be any that keep to these rules, and one draw needn't show every extreme that they name: `pair_key`: slot 0 of query block b is b, slots 1 and 2 are blocks (b - 1) mod 2048 and (b + 1) mod 2048; the 8 key blocks of a query block are distinct, and every key block k satisfies ((k // 8 - b // 8 + 3) mod (256)) <= 6. Only the first pair_count[b] slots of query block b are edges; some block uses all 8. The real nodes of a block are its first node_count entries; some block is full.
All inputs are finite; a program needn't handle non-finite values.
Results may differ from the reference program's by a relative error of at most 0.0061.
Values may be sent and summed in bfloat16 or wider, within the bound.
A program may use at most 32 MiB of HBM per device.

```python
import jax
import jax.numpy as jnp
from jax import lax

D = 512
HEADS = 8
HEAD_DIM = 64
BLOCK = 64
KSLOTS = 8
SPAN = 3
BLK_DEV = 8
NBLK = 2048
NODES = 131072
N_BLK = 256


def draw_x_nodes(key, part):
    first = jax.random.fold_in(key, 0)
    base = jax.random.truncated_normal(first, -6.0, 6.0, (NODES, D), jnp.float32)
    return base.astype(jnp.bfloat16)


def draw_w_qkv(key, part):
    first = jax.random.fold_in(key, 0)
    base = jax.random.truncated_normal(first, -6.0, 6.0, (D, 3, D), jnp.float32) * D ** (-0.5)
    return base.astype(jnp.bfloat16)


def draw_pair_key(key, part):
    width = (2 * SPAN + 1) * BLK_DEV
    cycle = NBLK // BLK_DEV
    query = jnp.arange(NBLK, dtype=jnp.int32)[:, None]
    cand = jnp.arange(width, dtype=jnp.int32)[None, :]
    device = query // BLK_DEV
    blocks = (device + cand // BLK_DEV - SPAN) % cycle * BLK_DEV + cand % BLK_DEV
    centre = SPAN * BLK_DEV + query % BLK_DEV
    prio = jax.random.randint(key, (NBLK, width), 0, 2 ** 20, jnp.int32) * width + cand
    prio = jnp.where(cand == centre, 2 ** 30, prio)
    prio = jnp.where(cand == centre - 1, 2 ** 30 - 1, prio)
    prio = jnp.where(cand == centre + 1, 2 ** 30 - 2, prio)
    chosen = lax.top_k(prio, KSLOTS)[1]
    return jnp.take_along_axis(blocks, chosen, axis=1).astype(jnp.int32)


def draw_pair_count(key, part):
    first, second = jax.random.split(jax.random.fold_in(key, 7), 2)
    counts = jax.random.randint(first, (NBLK,), 3, KSLOTS + 1, jnp.int32)
    spot = jax.random.randint(second, (), 0, NBLK, jnp.int32)
    return counts.at[spot].set(KSLOTS)


def draw_node_count(key, part):
    first, second = jax.random.split(jax.random.fold_in(key, 11), 2)
    counts = jax.random.randint(first, (NBLK,), 16, BLOCK + 1, jnp.int32)
    spot = jax.random.randint(second, (), 0, NBLK, jnp.int32)
    return counts.at[spot].set(BLOCK)


def block_scale(key, shape, cuts, low, high):
    factor_of, own = 1.0, jax.random.fold_in(key, 6)
    for axis_at, shards_of in cuts:
        heights = jnp.exp(jax.random.uniform(jax.random.fold_in(own, axis_at), (shards_of,), jnp.float32, low / len(cuts), high / len(cuts)))
        factor_of = factor_of * jnp.repeat(heights, shape[axis_at] // shards_of).reshape([-1 if axis == axis_at else 1 for axis in range(len(shape))])
    return factor_of


def centred(rng, dims, spread, limit, pieces=(), kind=jnp.bfloat16):
    loudness = block_scale(rng, dims, pieces, -0.22, 0.18) if pieces else 1.0
    array = jax.random.normal(rng, dims, jnp.float32) * spread * loudness
    return jnp.minimum(jnp.maximum(array, -limit), limit).astype(kind)


def setup_inputs(seed: int = 0) -> dict:
    key_list = jax.random.split(jax.random.key(seed), 7)
    x_nodes = draw_x_nodes(jax.random.fold_in(key_list[6], 71), 0)
    w_qkv = draw_w_qkv(jax.random.fold_in(key_list[6], 71), 0)
    w_out = centred(key_list[2], (D, D), D ** -0.5, 0.25, ((0, 4),))
    pair_key = draw_pair_key(jax.random.fold_in(key_list[6], 71), 0)
    pair_count = draw_pair_count(jax.random.fold_in(key_list[6], 71), 0)
    node_count = draw_node_count(jax.random.fold_in(key_list[6], 71), 0)
    return {"x_nodes": x_nodes, "w_qkv": w_qkv, "w_out": w_out, "pair_key": pair_key, "pair_count": pair_count, "node_count": node_count}


def reference(x_nodes, w_qkv, w_out, pair_key, pair_count, node_count):
    feats = x_nodes.astype(jnp.float32)
    normed = (feats * lax.rsqrt(lax.optimization_barrier(jnp.mean(feats * feats, axis=-1, keepdims=True)) + 1e-06)).astype(jnp.bfloat16)
    key_all = jnp.dot(normed, w_qkv[:, 1, :], preferred_element_type=jnp.float32).astype(jnp.bfloat16).reshape(NBLK, BLOCK, D)
    value_all = jnp.dot(normed, w_qkv[:, 2, :], preferred_element_type=jnp.float32).astype(jnp.bfloat16).reshape(NBLK, BLOCK, D)
    rows_grp = BLK_DEV * BLOCK
    scale = HEAD_DIM ** (-0.5)

    def group(index):
        start = (index * rows_grp).astype(jnp.int32)
        bstart = (index * BLK_DEV).astype(jnp.int32)
        rows = lax.dynamic_slice_in_dim(normed, start, rows_grp, 0)
        query = jnp.dot(rows, w_qkv[:, 0, :], preferred_element_type=jnp.float32).astype(jnp.bfloat16)
        query = query.reshape(BLK_DEV, BLOCK, HEADS, HEAD_DIM)
        keyb = lax.dynamic_slice_in_dim(pair_key, bstart, BLK_DEV, 0)
        used = lax.dynamic_slice_in_dim(pair_count, bstart, BLK_DEV, 0)
        keys = key_all[keyb].reshape(BLK_DEV, KSLOTS * BLOCK, HEADS, HEAD_DIM)
        values = value_all[keyb].reshape(BLK_DEV, KSLOTS * BLOCK, HEADS, HEAD_DIM)
        counts = node_count[keyb]
        slot_ok = jnp.arange(KSLOTS, dtype=jnp.int32)[None, :] < used[:, None]
        node_ok = jnp.arange(BLOCK, dtype=jnp.int32)[None, None, :] < counts[:, :, None]
        valid = (slot_ok[:, :, None] & node_ok).reshape(BLK_DEV, 1, 1, KSLOTS * BLOCK)
        scores = jnp.einsum('bqhd,bkhd->bhqk', query.astype(jnp.float32), keys.astype(jnp.float32)) * scale
        top = lax.optimization_barrier(jnp.max(jnp.where(valid, scores, -1e+30), axis=-1, keepdims=True))
        expo = jnp.exp(jnp.where(valid, scores - top, -1e+30))
        weights = (expo / lax.optimization_barrier(jnp.sum(expo, axis=-1, keepdims=True))).astype(jnp.bfloat16)
        attended = jnp.einsum('bhqk,bkhd->bqhd', weights.astype(jnp.float32), values.astype(jnp.float32))
        attended = attended.astype(jnp.bfloat16).reshape(rows_grp, D)
        term = jnp.dot(attended, w_out, preferred_element_type=jnp.float32)
        own = lax.dynamic_slice_in_dim(x_nodes, start, rows_grp, 0).astype(jnp.float32)
        return (own + term).astype(jnp.bfloat16)
    result = lax.map(group, jnp.arange(N_BLK, dtype=jnp.int32))
    return result.reshape(NODES, D)
```

```python
import functools

import jax
import jax.numpy as jnp
from jax import lax
from jax.experimental import pallas as pl
from jax.experimental.pallas import tpu as pltpu
from jax.sharding import PartitionSpec as P

HEAD_DIM = 64
BLOCK = 64
KSLOTS = 8
LANES = 128
REPS = 4
ROWS = 512
BLK_DEV = 8
SLOTS = 16
PIECES = 2
PIECE_ROWS = ROWS // PIECES
PARTS = 4
PART_BLOCKS = BLK_DEV // PARTS
PART_ROWS = ROWS // PARTS
NEG = -1e30
MESH = pl.DeviceIdType.MESH


def kernel(
    n_blk,
    x_ref,
    w_ref,
    wo_ref,
    key_ref,
    used_ref,
    node_ref,
    out_ref,
    xbuf,
    kv,
    qbuf,
    wbuf,
    wobuf,
    owobuf,
    att,
    oatt,
    tsend,
    trecv,
    usend,
    urecv,
    local_sem,
    ahead_sem,
    back_sem,
    recv_sem,
    ksend_sem,
    krecv_sem,
    wo_sem,
    att_sem,
    t_sem,
    u_sem,
):
    blk = lax.axis_index("blk")
    rep = lax.axis_index("rep")
    core = lax.rem(blk, 2)
    is_last = lax.div(rep, 3)
    is_first = lax.div(3 - rep, 3)
    inner = lax.rem(lax.div(rep + 1, 2), 2)
    ahead = (lax.rem(blk + 2 * is_last, n_blk), lax.rem(rep + 1, REPS))
    back = (lax.rem(blk + n_blk - 2 * is_first, n_blk), lax.rem(rep + 3, REPS))
    sibling = (blk + 1 - 2 * core, rep)
    mate_rep = rep + 1 - 2 * lax.rem(rep, 2)
    peer_rep = 3 - rep
    mate = (blk, mate_rep)
    peer = (blk, lax.rem(peer_rep, REPS))
    own = rep + 4 + 4 * core

    loads = [
        pltpu.make_async_copy(x_ref, xbuf.at[own], local_sem.at[0]),
        pltpu.make_async_copy(w_ref, wbuf, local_sem.at[1]),
    ] + [
        pltpu.make_async_copy(
            wo_ref.at[:, pl.ds(LANES * d, LANES)], wobuf.at[d], local_sem.at[2 + d]
        )
        for d in range(REPS)
    ]
    for load in loads:
        load.start()

    barrier = pltpu.get_barrier_semaphore()
    for other in (ahead, back, sibling):
        pl.semaphore_signal(barrier, inc=1, device_id=other, device_id_type=MESH)
    pl.semaphore_wait(barrier, 3)

    def shard_copy(slot, piece, forward, source=None):
        rows = pl.ds(piece * PIECE_ROWS, PIECE_ROWS)
        target = slot - 4 * is_last if forward else slot + 4 * is_first
        return pltpu.make_async_remote_copy(
            src_ref=xbuf.at[slot, rows] if source is None else source.at[rows],
            dst_ref=xbuf.at[target, rows],
            send_sem=(ahead_sem if forward else back_sem).at[slot, piece],
            recv_sem=recv_sem.at[target, piece],
            device_id=ahead if forward else back,
            device_id_type=MESH,
        )

    def arrived(slot, piece):
        rows = pl.ds(piece * PIECE_ROWS, PIECE_ROWS)
        pltpu.make_async_remote_copy(
            src_ref=xbuf.at[slot, rows],
            dst_ref=xbuf.at[slot, rows],
            send_sem=ahead_sem.at[slot, piece],
            recv_sem=recv_sem.at[slot, piece],
            device_id=ahead,
            device_id_type=MESH,
        ).wait_recv()

    for piece in range(PIECES):
        shard_copy(own, piece, True, x_ref).start()
        shard_copy(own, piece, False, x_ref).start()

    def relay(step, carry):
        for piece in range(PIECES):
            low = own - step
            high = own + step

            @pl.when(low >= 0)
            def _():
                arrived(low, piece)

                @pl.when(low - 4 * is_last >= 0)
                def _():
                    shard_copy(low, piece, True).start()

            @pl.when(high < SLOTS)
            def _():
                arrived(high, piece)

                @pl.when(high + 4 * is_first < SLOTS)
                def _():
                    shard_copy(high, piece, False).start()

        return carry

    def projected(run, half, weights):
        rows = pl.ds(half * (ROWS // 2), ROWS // 2)
        shards = [xbuf[4 * run + i, rows] for i in range(REPS)]
        squares = jnp.zeros((ROWS // 2, LANES), jnp.float32)
        for shard in shards:
            wide = shard.astype(jnp.float32)
            squares += wide * wide
        mean = jnp.sum(squares, axis=1, keepdims=True) * (1.0 / (REPS * LANES))
        whole = jnp.concatenate(shards, axis=1)
        product = jnp.dot(whole, weights, preferred_element_type=jnp.float32)
        return product * lax.rsqrt(mean + 1e-06)

    def window_of(run):
        return lax.rem(2 * run + 9 - 2 * core, 8)

    def kv_copy(run):
        place = window_of(run)
        there = lax.rem(place + 7 + 2 * core, 8)
        return pltpu.make_async_remote_copy(
            src_ref=kv.at[place],
            dst_ref=kv.at[there],
            send_sem=ksend_sem.at[run],
            recv_sem=krecv_sem.at[lax.div(there, 2)],
            device_id=sibling,
            device_id_type=MESH,
        )

    def make_kv(run, with_query):
        place = window_of(run)
        parts = [wbuf[1], wbuf[2]] + ([wbuf[0]] if with_query else [])
        weights = jnp.concatenate(parts, axis=1)

        def one(half, carry):
            values = projected(run, half, weights)
            count = BLK_DEV // 2
            blocks = pl.ds(half * count, count)
            for which in range(2):
                piece = values[:, which * LANES : (which + 1) * LANES]
                kv[place, which, blocks] = piece.astype(jnp.bfloat16).reshape(count, BLOCK, LANES)
            if with_query:
                piece = values[:, 2 * LANES :] * HEAD_DIM ** (-0.5)
                qbuf[blocks] = piece.astype(jnp.bfloat16).reshape(count, BLOCK, LANES)
            return carry

        lax.fori_loop(0, 2, one, 0)
        kv_copy(run).start()

    lax.fori_loop(1, 4, relay, 0)
    for load in loads:
        load.wait()

    def wo_copy():
        return pltpu.make_async_remote_copy(
            src_ref=wobuf,
            dst_ref=owobuf,
            send_sem=wo_sem.at[0],
            recv_sem=wo_sem.at[1],
            device_id=mate,
            device_id_type=MESH,
        )

    @pl.when(inner == 0)
    def _():
        wo_copy().start()

    make_kv(1 + core, True)
    lax.fori_loop(4, 8, relay, 0)
    make_kv(core, False)
    lax.fori_loop(8, 9, relay, 0)
    make_kv(2 + core, False)
    lax.fori_loop(9, 12, relay, 0)
    make_kv(3 - 3 * core, False)

    for place in range(4):
        pltpu.make_async_remote_copy(
            src_ref=kv.at[2 * place],
            dst_ref=kv.at[2 * place],
            send_sem=ksend_sem.at[place],
            recv_sem=krecv_sem.at[place],
            device_id=sibling,
            device_id_type=MESH,
        ).wait_recv()

    def attend(index, carry):
        query = qbuf[index]
        lane = lax.broadcasted_iota(jnp.int32, (BLOCK, LANES), 1)
        left = lane < HEAD_DIM
        zero = jnp.zeros_like(query)
        both = jnp.concatenate(
            [jnp.where(left, query, zero), jnp.where(left, zero, query)], axis=0
        )
        used = used_ref[index]
        keys, values, counts = [], [], []
        for slot in range(KSLOTS):
            key = key_ref[index, slot]
            place = lax.rem(lax.div(key, BLK_DEV) - blk + 3 + n_blk, n_blk) & 7
            inside = lax.rem(key, BLK_DEV)
            keys.append(kv[place, 0, inside])
            values.append(kv[place, 1, inside])
            counts.append(jnp.where(slot < used, node_ref[key], 0))
        row_lane = lax.broadcasted_iota(jnp.int32, (1, LANES), 1)
        bias = []
        for pair in range(KSLOTS // 2):
            limit = jnp.where(row_lane < BLOCK, counts[2 * pair], counts[2 * pair + 1] + BLOCK)
            bias.append(jnp.where(row_lane < limit, 0.0, NEG))
        bias = jnp.concatenate(bias, axis=1)
        scores = lax.dot_general(
            both,
            jnp.concatenate(keys, axis=0),
            (((1,), (1,)), ((), ())),
            preferred_element_type=jnp.float32,
        )
        scores = scores + bias
        top = jnp.max(scores, axis=1, keepdims=True)
        expo = jnp.exp(scores - top)
        total = jnp.sum(expo, axis=1, keepdims=True)
        mixed = jnp.dot(
            expo.astype(jnp.bfloat16),
            jnp.concatenate(values, axis=0),
            preferred_element_type=jnp.float32,
        )
        mixed = mixed / total
        att[pl.ds(index * BLOCK, BLOCK), :] = jnp.where(
            left, mixed[:BLOCK], mixed[BLOCK:]
        ).astype(jnp.bfloat16)
        return carry

    def att_copy(part):
        rows = pl.ds(part * PART_ROWS, PART_ROWS)
        return pltpu.make_async_remote_copy(
            src_ref=att.at[rows],
            dst_ref=oatt.at[rows],
            send_sem=att_sem.at[0, part],
            recv_sem=att_sem.at[1, part],
            device_id=mate,
            device_id_type=MESH,
        )

    def t_copy(part):
        return pltpu.make_async_remote_copy(
            src_ref=tsend.at[part],
            dst_ref=trecv.at[part],
            send_sem=t_sem.at[0, part],
            recv_sem=t_sem.at[1, part],
            device_id=peer,
            device_id_type=MESH,
        )

    def u_copy(part):
        return pltpu.make_async_remote_copy(
            src_ref=usend.at[part],
            dst_ref=urecv.at[part],
            send_sem=u_sem.at[0, part],
            recv_sem=u_sem.at[1, part],
            device_id=mate,
            device_id_type=MESH,
        )

    def two_rows(part):
        rows = pl.ds(part * PART_ROWS, PART_ROWS)
        return jnp.concatenate([att[rows], oatt[rows]], axis=1)

    def two_weights(column):
        return jnp.concatenate([wobuf[column], owobuf[column]], axis=0)

    def send_terms(part):
        att_copy(part).wait_recv()
        held = two_rows(part)
        for which, column in enumerate((peer_rep, 3 - mate_rep)):
            term = jnp.dot(held, two_weights(column), preferred_element_type=jnp.float32)
            tsend[part, which] = term.astype(jnp.bfloat16)
        t_copy(part).start()

    @pl.when(inner == 1)
    def _():
        wo_copy().wait_recv()

    def attention_part(part, carry):
        lax.fori_loop(part * PART_BLOCKS, (part + 1) * PART_BLOCKS, attend, 0)

        @pl.when(inner == 0)
        def _():
            att_copy(part).start()

        @pl.when((inner == 1) & (part > 0))
        def _():
            send_terms(part - 1)

        return carry

    lax.fori_loop(0, PARTS, attention_part, 0)

    @pl.when(inner == 1)
    def _():
        send_terms(PARTS - 1)

        def finish(part, carry):
            rows = pl.ds(part * PART_ROWS, PART_ROWS)
            mine = jnp.dot(two_rows(part), two_weights(rep), preferred_element_type=jnp.float32)
            mine = mine + xbuf[own, rows].astype(jnp.float32)
            passed = jnp.dot(att[rows], wobuf[mate_rep], preferred_element_type=jnp.float32)
            t_copy(part).wait_recv()
            usend[part] = (passed + trecv[part, 1].astype(jnp.float32)).astype(jnp.bfloat16)
            u_copy(part).start()
            out_ref[rows, :] = (mine + trecv[part, 0].astype(jnp.float32)).astype(jnp.bfloat16)
            return carry

        lax.fori_loop(0, PARTS, finish, 0)
        for part in range(PARTS):
            t_copy(part).wait_send()
            u_copy(part).wait_send()

    @pl.when(inner == 0)
    def _():
        def finish(part, carry):
            rows = pl.ds(part * PART_ROWS, PART_ROWS)
            mine = jnp.dot(att[rows], wobuf[rep], preferred_element_type=jnp.float32)
            mine = mine + xbuf[own, rows].astype(jnp.float32)
            u_copy(part).wait_recv()
            out_ref[rows, :] = (mine + urecv[part].astype(jnp.float32)).astype(jnp.bfloat16)
            return carry

        lax.fori_loop(0, PARTS, finish, 0)
        for part in range(PARTS):
            att_copy(part).wait_send()
        wo_copy().wait_send()

    for run in range(4):
        kv_copy(run).wait_send()

    def drain(step, carry):
        for piece in range(PIECES):

            @pl.when(own - step - 4 * is_last >= 0)
            def _():
                shard_copy(own - step, piece, True).wait_send()

            @pl.when(own + step + 4 * is_first < SLOTS)
            def _():
                shard_copy(own + step, piece, False).wait_send()

        return carry

    lax.fori_loop(0, 12, drain, 0)


def body(x_nodes, w_qkv, w_out, pair_key, pair_count, node_count):
    n_blk = lax.axis_size("blk")
    weights = jnp.transpose(w_qkv, (1, 0, 2))
    bf16 = jnp.bfloat16
    vmem = pltpu.VMEM
    dma = pltpu.SemaphoreType.DMA
    return pl.pallas_call(
        functools.partial(kernel, n_blk),
        out_shape=jax.ShapeDtypeStruct((ROWS, LANES), bf16),
        in_specs=[pl.BlockSpec(memory_space=pl.ANY)] * 3
        + [pl.BlockSpec(memory_space=pltpu.SMEM)] * 3,
        out_specs=pl.BlockSpec(memory_space=pltpu.VMEM),
        scratch_shapes=[
            vmem((SLOTS, ROWS, LANES), bf16),
            vmem((8, 2, BLK_DEV, BLOCK, LANES), bf16),
            vmem((BLK_DEV, BLOCK, LANES), bf16),
            vmem((3, REPS * LANES, LANES), bf16),
            vmem((REPS, LANES, LANES), bf16),
            vmem((REPS, LANES, LANES), bf16),
            vmem((ROWS, LANES), bf16),
            vmem((ROWS, LANES), bf16),
            vmem((PARTS, 2, PART_ROWS, LANES), bf16),
            vmem((PARTS, 2, PART_ROWS, LANES), bf16),
            vmem((PARTS, PART_ROWS, LANES), bf16),
            vmem((PARTS, PART_ROWS, LANES), bf16),
            dma((2 + REPS,)),
            dma((SLOTS, PIECES)),
            dma((SLOTS, PIECES)),
            dma((SLOTS, PIECES)),
            dma((4,)),
            dma((4,)),
            dma((2,)),
            dma((2, PARTS)),
            dma((2, PARTS)),
            dma((2, PARTS)),
        ],
        compiler_params=pltpu.CompilerParams(
            collective_id=0, has_side_effects=True, vmem_limit_bytes=40 << 20
        ),
        name="graph_layer",
    )(x_nodes, weights, w_out, pair_key, pair_count, node_count)


def solution(mesh):
    return jax.shard_map(
        body,
        mesh=mesh,
        in_specs=(
            P("blk", "rep"),
            P(None, None, "rep"),
            P("rep", None),
            P("blk", None),
            P("blk"),
            P(),
        ),
        out_specs=P("blk", "rep"),
        check_vma=False,
    )
```

```python
import functools

import jax
import jax.numpy as jnp
from jax import lax
from jax.experimental import pallas as pl
from jax.experimental.pallas import tpu as pltpu
from jax.sharding import PartitionSpec as P

HEAD_DIM = 64
BLOCK = 64
KSLOTS = 8
LANES = 128
REPS = 4
ROWS = 512
BLK_DEV = 8
LONG = 12
SHORT = 8
PIECES = 4
PIECE_ROWS = ROWS // PIECES
PARTS = 4
PART_BLOCKS = BLK_DEV // PARTS
PART_ROWS = ROWS // PARTS
STRIP = 128
NEG = -1e30
MESH = pl.DeviceIdType.MESH
bf16 = jnp.bfloat16
f32 = jnp.float32


def kernel(
    n_blk,
    x_ref,
    w_ref,
    wo_ref,
    key_hbm,
    used_hbm,
    node_hbm,
    out_ref,
    xlong,
    xshort,
    kv,
    qbuf,
    wbuf,
    wobuf,
    owobuf,
    att,
    oatt,
    tsend,
    trecv,
    usend,
    urecv,
    frecv,
    key_ref,
    used_ref,
    node_ref,
    local_sem,
    cross_sem,
    lsend_sem,
    ssend_sem,
    lrecv_sem,
    srecv_sem,
    give_sem,
    take_sem,
    ksend_sem,
    krecv_sem,
    wo_sem,
    att_sem,
    t_sem,
    f_sem,
    u_sem,
):
    blk = lax.axis_index("blk")
    rep = lax.axis_index("rep")
    core = lax.rem(blk, 2)
    at = rep + core * (3 - 2 * rep)
    at_end = lax.div(at, 3)
    at_start = lax.div(3 - at, 3)
    sign = 1 - 2 * core
    down_blk = lax.rem(blk + n_blk + 2 * sign * at_end, n_blk)
    up_blk = lax.rem(blk + n_blk - 2 * sign * at_start, n_blk)
    down_rep = lax.rem(rep + REPS + sign, REPS)
    up_rep = lax.rem(rep + REPS - sign, REPS)
    down = (down_blk, down_rep)
    up = (up_blk, up_rep)
    cross = (up_blk + sign, up_rep)
    sibling = (blk + sign, rep)
    inner = lax.rem(lax.div(rep + 1, 2), 2)
    mate_rep = rep + 1 - 2 * lax.rem(rep, 2)
    peer_rep = 3 - rep
    far_rep = lax.rem(rep + 2, REPS)
    mate = (blk, mate_rep)
    peer = (blk, peer_rep)
    far = (blk, far_rep)

    barrier = pltpu.get_barrier_semaphore()
    for other in (down, up, cross, sibling, far):
        pl.semaphore_signal(barrier, inc=1, device_id=other, device_id_type=MESH)

    loads = [
        pltpu.make_async_copy(x_ref, xshort.at[4 + at], local_sem.at[0]),
        pltpu.make_async_copy(w_ref, wbuf, local_sem.at[1]),
        pltpu.make_async_copy(key_hbm, key_ref, local_sem.at[2]),
        pltpu.make_async_copy(used_hbm, used_ref, local_sem.at[3]),
        pltpu.make_async_copy(node_hbm, node_ref, local_sem.at[4]),
    ] + [
        pltpu.make_async_copy(
            wo_ref.at[:, pl.ds(LANES * d, LANES)], wobuf.at[d], local_sem.at[5 + d]
        )
        for d in range(REPS)
    ]
    for load in loads:
        load.start()
    pl.semaphore_wait(barrier, 5)

    def remote(source, target, send_sem, recv_sem, device):
        return pltpu.make_async_remote_copy(
            src_ref=source,
            dst_ref=target,
            send_sem=send_sem,
            recv_sem=recv_sem,
            device_id=device,
            device_id_type=MESH,
        )

    def piece_rows(piece):
        return pl.ds(piece * PIECE_ROWS, PIECE_ROWS)

    def cross_copy(piece):
        slot = 11 - at - 4 * at_start
        rows = piece_rows(piece)
        return remote(
            x_ref.at[rows],
            xlong.at[slot, rows],
            cross_sem.at[piece],
            lrecv_sem.at[slot, piece],
            cross,
        )

    def long_copy(slot, piece):
        rows = piece_rows(piece)
        there = slot - 4 * at_end
        return remote(
            xlong.at[slot, rows],
            xlong.at[there, rows],
            lsend_sem.at[slot, piece],
            lrecv_sem.at[there, piece],
            down,
        )

    def short_copy(slot, piece, source=None):
        rows = piece_rows(piece)
        there = slot - 4 * at_end
        return remote(
            xshort.at[slot, rows] if source is None else source.at[rows],
            xshort.at[there, rows],
            ssend_sem.at[slot, piece],
            srecv_sem.at[there, piece],
            down,
        )

    def give_copy(step, piece):
        rows = piece_rows(piece)
        there = 3 - at + step
        return remote(
            xlong.at[8 + at - step, rows],
            xshort.at[4 + there, rows],
            give_sem.at[step - 1, piece],
            take_sem.at[there, piece],
            sibling,
        )

    for piece in range(PIECES):
        cross_copy(piece).start()
        short_copy(4 + at, piece, x_ref).start()

    def poll_long(step):
        slot = 8 + at - step

        def one(piece, carry):
            @pl.when(slot >= 0)
            def _():
                rows = piece_rows(piece)
                remote(
                    xlong.at[slot, rows],
                    xlong.at[slot, rows],
                    lsend_sem.at[slot, piece],
                    lrecv_sem.at[slot, piece],
                    down,
                ).wait_recv()

                @pl.when(slot - 4 * at_end >= 0)
                def _():
                    long_copy(slot, piece).start()

            if step <= 3:

                @pl.when(at >= step)
                def _():
                    give_copy(step, piece).start()

            return carry

        lax.fori_loop(0, PIECES, one, 0)

    def poll_short(step):
        slot = 4 + at - step

        def one(piece, carry):
            @pl.when(slot >= 0)
            def _():
                rows = piece_rows(piece)
                remote(
                    xshort.at[slot, rows],
                    xshort.at[slot, rows],
                    ssend_sem.at[slot, piece],
                    srecv_sem.at[slot, piece],
                    down,
                ).wait_recv()

                @pl.when(slot - 4 * at_end >= 0)
                def _():
                    short_copy(slot, piece).start()

            return carry

        lax.fori_loop(0, PIECES, one, 0)

    def project(chain, run, place, strip, with_query=False):
        rows = pl.ds(strip * STRIP, STRIP)
        shards = [chain[4 * run + i + core * (3 - 2 * i), rows] for i in range(REPS)]
        squares = jnp.zeros((STRIP, LANES), f32)
        for shard in shards:
            wide = shard.astype(f32)
            squares += wide * wide
        mean = jnp.sum(squares, axis=1, keepdims=True) * (1.0 / (REPS * LANES))
        whole = jnp.concatenate(shards, axis=1)
        parts = [wbuf[1], wbuf[2]] + ([wbuf[0]] if with_query else [])
        weights = jnp.concatenate(parts, axis=1)
        product = jnp.dot(whole, weights, preferred_element_type=f32)
        product = product * lax.rsqrt(mean + 1e-06)
        count = STRIP // BLOCK
        blocks = pl.ds(strip * count, count)
        for which in range(2):
            piece = product[:, which * LANES : (which + 1) * LANES]
            kv[place, which, blocks] = piece.astype(bf16).reshape(count, BLOCK, LANES)
        if with_query:
            piece = product[:, 2 * LANES :] * HEAD_DIM ** (-0.5)
            qbuf[blocks] = piece.astype(bf16).reshape(count, BLOCK, LANES)

    def project_all(chain, run, place, with_query=False):
        def one(strip, carry):
            project(chain, run, place, strip, with_query)
            return carry

        lax.fori_loop(0, ROWS // STRIP, one, 0)

    def kv_copy(index):
        place = 3 - sign * index
        there = place - sign
        return remote(
            kv.at[place], kv.at[there], ksend_sem.at[index], krecv_sem.at[index], sibling
        )

    def wo_copy():
        return remote(wobuf, owobuf, wo_sem.at[0], wo_sem.at[1], mate)

    poll_long(1)
    poll_short(1)
    poll_long(2)
    poll_short(2)
    poll_long(3)
    poll_short(3)
    poll_long(4)
    for load in loads:
        load.wait()

    @pl.when(inner == 0)
    def _():
        wo_copy().start()

    for there in range(1, REPS):

        def one(piece, carry):
            @pl.when(there > at)
            def _():
                rows = piece_rows(piece)
                remote(
                    xlong.at[0, rows],
                    xshort.at[4 + there, rows],
                    give_sem.at[0, piece],
                    take_sem.at[there, piece],
                    sibling,
                ).wait_recv()

            return carry

        lax.fori_loop(0, PIECES, one, 0)
    project_all(xshort, 1, 3, True)
    kv_copy(0).start()
    poll_short(4)
    poll_long(5)
    poll_long(6)
    poll_short(5)
    poll_long(7)
    project_all(xlong, 1, 3 - sign, False)
    kv_copy(1).start()
    poll_short(6)
    poll_long(8)
    poll_short(7)
    poll_long(9)
    project_all(xshort, 0, 3 - 2 * sign, False)
    kv_copy(2).start()
    poll_long(10)
    poll_long(11)
    project_all(xlong, 0, 3 - 3 * sign, False)

    for index in range(3):
        kv_copy(index).wait_recv()

    def attend(index):
        query = qbuf[index]
        lane = lax.broadcasted_iota(jnp.int32, (BLOCK, LANES), 1)
        left = lane < HEAD_DIM
        zero = jnp.zeros_like(query)
        both = jnp.concatenate(
            [jnp.where(left, query, zero), jnp.where(left, zero, query)], axis=0
        )
        used = used_ref[index]
        keys, values, counts = [], [], []
        for slot in range(KSLOTS):
            key = key_ref[index, slot]
            place = lax.rem(lax.div(key, BLK_DEV) - blk + 3 + n_blk, n_blk) & 7
            inside = lax.rem(key, BLK_DEV)
            keys.append(kv[place, 0, inside])
            values.append(kv[place, 1, inside])
            counts.append(jnp.where(slot < used, node_ref[key], 0))
        row_lane = lax.broadcasted_iota(jnp.int32, (1, LANES), 1)
        bias = []
        for pair in range(KSLOTS // 2):
            limit = jnp.where(row_lane < BLOCK, counts[2 * pair], counts[2 * pair + 1] + BLOCK)
            bias.append(jnp.where(row_lane < limit, 0.0, NEG))
        bias = jnp.concatenate(bias, axis=1)
        scores = lax.dot_general(
            both,
            jnp.concatenate(keys, axis=0),
            (((1,), (1,)), ((), ())),
            preferred_element_type=jnp.float32,
        )
        scores = scores + bias
        top = jnp.max(scores, axis=1, keepdims=True)
        expo = jnp.exp(scores - top)
        total = jnp.sum(expo, axis=1, keepdims=True)
        mixed = jnp.dot(
            expo.astype(jnp.bfloat16),
            jnp.concatenate(values, axis=0),
            preferred_element_type=jnp.float32,
        )
        mixed = mixed / total
        att[pl.ds(index * BLOCK, BLOCK), :] = jnp.where(
            left, mixed[:BLOCK], mixed[BLOCK:]
        ).astype(jnp.bfloat16)

    def part_rows(part):
        return pl.ds(part * PART_ROWS, PART_ROWS)

    def att_copy(part):
        rows = part_rows(part)
        return remote(att.at[rows], oatt.at[rows], att_sem.at[0, part], att_sem.at[1, part], mate)

    def u_copy(part):
        return remote(usend.at[part], urecv.at[part], u_sem.at[0, part], u_sem.at[1, part], mate)

    def far_copy(part):
        return remote(
            tsend.at[part, 0], frecv.at[part], f_sem.at[0, part], f_sem.at[1, part], far
        )

    def peer_copy(part):
        return remote(
            tsend.at[part, 1], trecv.at[part], t_sem.at[0, part], t_sem.at[1, part], peer
        )

    def two_rows(part):
        rows = part_rows(part)
        return jnp.concatenate([att[rows], oatt[rows]], axis=1)

    def two_weights(column):
        return jnp.concatenate([wobuf[column], owobuf[column]], axis=0)

    def send_terms(part):
        att_copy(part).wait_recv()
        held = two_rows(part)
        for which, column, copy in ((0, far_rep, far_copy), (1, peer_rep, peer_copy)):
            term = jnp.dot(held, two_weights(column), preferred_element_type=f32)
            tsend[part, which] = term.astype(bf16)
            copy(part).start()

    @pl.when(inner == 1)
    def _():
        wo_copy().wait_recv()

    def attention_part(part, carry):
        for index in range(PART_BLOCKS):
            attend(part * PART_BLOCKS + index)

        @pl.when(inner == 0)
        def _():
            att_copy(part).start()

        @pl.when(inner == 1)
        def _():
            term = jnp.dot(att[part_rows(part)], wobuf[mate_rep], preferred_element_type=f32)
            usend[part] = term.astype(bf16)
            u_copy(part).start()

            @pl.when(part > 0)
            def _():
                send_terms(part - 1)

        return carry

    lax.fori_loop(0, PARTS, attention_part, 0)

    def residual(part):
        return xshort[4 + at, part_rows(part)].astype(f32)

    @pl.when(inner == 1)
    def _():
        send_terms(PARTS - 1)

        def finish(part, carry):
            mine = jnp.dot(two_rows(part), two_weights(rep), preferred_element_type=f32)
            mine = mine + residual(part)
            peer_copy(part).wait_recv()
            out_ref[part_rows(part), :] = (mine + trecv[part].astype(f32)).astype(bf16)
            return carry

        lax.fori_loop(0, PARTS, finish, 0)
        for part in range(PARTS):
            u_copy(part).wait_send()
            far_copy(part).wait_send()
            peer_copy(part).wait_send()

    @pl.when(inner == 0)
    def _():
        def finish(part, carry):
            mine = jnp.dot(att[part_rows(part)], wobuf[rep], preferred_element_type=f32)
            mine = mine + residual(part)
            u_copy(part).wait_recv()
            mine = mine + urecv[part].astype(f32)
            far_copy(part).wait_recv()
            out_ref[part_rows(part), :] = (mine + frecv[part].astype(f32)).astype(bf16)
            return carry

        lax.fori_loop(0, PARTS, finish, 0)
        for part in range(PARTS):
            att_copy(part).wait_send()
        wo_copy().wait_send()

    for index in range(3):
        kv_copy(index).wait_send()

    def drain(piece, carry):
        cross_copy(piece).wait_send()

        def long_one(slot, carry):
            @pl.when((slot < 8 + at) & (slot - 4 * at_end >= 0))
            def _():
                long_copy(slot, piece).wait_send()

            return carry

        def short_one(slot, carry):
            @pl.when((slot < 5 + at) & (slot - 4 * at_end >= 0))
            def _():
                short_copy(slot, piece).wait_send()

            return carry

        lax.fori_loop(0, LONG, long_one, 0)
        lax.fori_loop(0, SHORT, short_one, 0)
        for step in range(1, REPS):

            @pl.when(at >= step)
            def _():
                give_copy(step, piece).wait_send()

        return carry

    lax.fori_loop(0, PIECES, drain, 0)


def body(x_nodes, w_qkv, w_out, pair_key, pair_count, node_count):
    n_blk = lax.axis_size("blk")
    weights = jnp.transpose(w_qkv, (1, 0, 2))
    vmem = pltpu.VMEM
    dma = pltpu.SemaphoreType.DMA
    return pl.pallas_call(
        functools.partial(kernel, n_blk),
        out_shape=jax.ShapeDtypeStruct((ROWS, LANES), bf16),
        in_specs=[pl.BlockSpec(memory_space=pl.ANY)] * 6,
        out_specs=pl.BlockSpec(memory_space=pltpu.VMEM),
        scratch_shapes=[
            vmem((LONG, ROWS, LANES), bf16),
            vmem((SHORT, ROWS, LANES), bf16),
            vmem((8, 2, BLK_DEV, BLOCK, LANES), bf16),
            vmem((BLK_DEV, BLOCK, LANES), bf16),
            vmem((3, REPS * LANES, LANES), bf16),
            vmem((REPS, LANES, LANES), bf16),
            vmem((REPS, LANES, LANES), bf16),
            vmem((ROWS, LANES), bf16),
            vmem((ROWS, LANES), bf16),
            vmem((PARTS, 2, PART_ROWS, LANES), bf16),
            vmem((PARTS, PART_ROWS, LANES), bf16),
            vmem((PARTS, PART_ROWS, LANES), bf16),
            vmem((PARTS, PART_ROWS, LANES), bf16),
            vmem((PARTS, PART_ROWS, LANES), bf16),
            pltpu.SMEM(pair_key.shape, jnp.int32),
            pltpu.SMEM(pair_count.shape, jnp.int32),
            pltpu.SMEM(node_count.shape, jnp.int32),
            dma((5 + REPS,)),
            dma((PIECES,)),
            dma((LONG, PIECES)),
            dma((SHORT, PIECES)),
            dma((LONG, PIECES)),
            dma((SHORT, PIECES)),
            dma((3, PIECES)),
            dma((REPS, PIECES)),
            dma((3,)),
            dma((3,)),
            dma((2,)),
            dma((2, PARTS)),
            dma((2, PARTS)),
            dma((2, PARTS)),
            dma((2, PARTS)),
        ],
        compiler_params=pltpu.CompilerParams(
            collective_id=0, has_side_effects=True, vmem_limit_bytes=60 << 20
        ),
        name="graph_layer",
    )(x_nodes, weights, w_out, pair_key, pair_count, node_count)


def solution(mesh):
    return jax.shard_map(
        body,
        mesh=mesh,
        in_specs=(
            P("blk", "rep"),
            P(None, None, "rep"),
            P("rep", None),
            P("blk", None),
            P("blk"),
            P(),
        ),
        out_specs=P("blk", "rep"),
        check_vma=False,
    )
```

```python
import functools

import jax
import jax.numpy as jnp
from jax import lax
from jax.experimental import pallas as pl
from jax.experimental.pallas import tpu as pltpu
from jax.sharding import PartitionSpec as P

HEAD_DIM = 64
BLOCK = 64
KSLOTS = 8
LANES = 128
REPS = 4
ROWS = 512
BLK_DEV = 8
SLOTS = 12
LONG_STEPS = 8
SHORT_STEPS = 7
PIECES = 4
PIECE_ROWS = ROWS // PIECES
PARTS = 4
PART_BLOCKS = BLK_DEV // PARTS
PART_ROWS = ROWS // PARTS
STRIP = 128
STRIPS = ROWS // STRIP
def _order(text):
    found = []
    for word in text.split():
        kind = word.rstrip("0123456789.")
        number, _, piece = word[len(kind) :].partition(".")
        found.append((kind, int(number or 0), int(piece) if piece else None))
    return found


SCHEDULE = _order("""
L1 S1 L2 S2 L3 S3 L4 ready own0 S4 own1 L5 own2 S5 own3 L6 S6 L7 long0 long1 S7 long2 long3
short0 short1 short2 short3 L8.0 F.0 far0 L8.1 F.1 far1 L8.2 F.2 far2 L8.3 F.3 far3
""")
NEG = -1e30
MESH = pl.DeviceIdType.MESH
bf16 = jnp.bfloat16
f32 = jnp.float32


def kernel(
    n_blk,
    x_ref,
    w_ref,
    wo_ref,
    key_hbm,
    used_hbm,
    node_hbm,
    out_ref,
    xlong,
    xshort,
    kv,
    qbuf,
    wbuf,
    wobuf,
    owobuf,
    att,
    oatt,
    tsend,
    trecv,
    usend,
    urecv,
    frecv,
    key_ref,
    used_ref,
    node_ref,
    local_sem,
    cross_sem,
    lsend_sem,
    ssend_sem,
    lrecv_sem,
    srecv_sem,
    give_sem,
    far_give_sem,
    take_sem,
    ksend_sem,
    krecv_sem,
    wo_sem,
    att_sem,
    t_sem,
    f_sem,
    u_sem,
):
    blk = lax.axis_index("blk")
    rep = lax.axis_index("rep")
    core = lax.rem(blk, 2)
    at = rep + core * (3 - 2 * rep)
    at_end = lax.div(at, 3)
    at_start = lax.div(3 - at, 3)
    sign = 1 - 2 * core
    down_blk = lax.rem(blk + n_blk + 2 * sign * at_end, n_blk)
    up_blk = lax.rem(blk + n_blk - 2 * sign * at_start, n_blk)
    down_rep = lax.rem(rep + REPS + sign, REPS)
    up_rep = lax.rem(rep + REPS - sign, REPS)
    down = (down_blk, down_rep)
    up = (up_blk, up_rep)
    cross = (up_blk + sign, up_rep)
    sibling = (blk + sign, rep)
    inner = lax.rem(lax.div(rep + 1, 2), 2)
    mate_rep = rep + 1 - 2 * lax.rem(rep, 2)
    peer_rep = 3 - rep
    far_rep = lax.rem(rep + 2, REPS)
    drop_blk = lax.rem(blk + 6 * n_blk - 6 * sign * (at_end - at_start), n_blk)
    ends = at_end + at_start
    mate = (blk, mate_rep)
    peer = (blk, peer_rep)
    far = (blk, far_rep)

    barrier = pltpu.get_barrier_semaphore()
    for other in (down, up, cross, sibling, far):
        pl.semaphore_signal(barrier, inc=1, device_id=other, device_id_type=MESH)

    @pl.when(ends == 1)
    def _():
        pl.semaphore_signal(
            barrier,
            inc=1,
            device_id=(drop_blk, at_end * down_rep + at_start * up_rep),
            device_id_type=MESH,
        )

    loads = [
        pltpu.make_async_copy(x_ref, xshort.at[8 + at], local_sem.at[0]),
        pltpu.make_async_copy(w_ref, wbuf, local_sem.at[1]),
        pltpu.make_async_copy(key_hbm, key_ref, local_sem.at[2]),
        pltpu.make_async_copy(used_hbm, used_ref, local_sem.at[3]),
        pltpu.make_async_copy(node_hbm, node_ref, local_sem.at[4]),
    ] + [
        pltpu.make_async_copy(
            wo_ref.at[:, pl.ds(LANES * d, LANES)], wobuf.at[d], local_sem.at[5 + d]
        )
        for d in range(REPS)
    ]
    for load in loads:
        load.start()
    pl.semaphore_wait(barrier, 5 + ends)

    def remote(source, target, send_sem, recv_sem, device):
        return pltpu.make_async_remote_copy(
            src_ref=source,
            dst_ref=target,
            send_sem=send_sem,
            recv_sem=recv_sem,
            device_id=device,
            device_id_type=MESH,
        )

    def piece_rows(piece):
        return pl.ds(piece * PIECE_ROWS, PIECE_ROWS)

    def cross_copy(piece):
        slot = 11 - at - 4 * at_start
        rows = piece_rows(piece)
        return remote(
            x_ref.at[rows],
            xlong.at[slot, rows],
            cross_sem.at[piece],
            lrecv_sem.at[slot, piece],
            cross,
        )

    def long_copy(slot, piece):
        rows = piece_rows(piece)
        there = slot - 4 * at_end
        return remote(
            xlong.at[slot, rows],
            xlong.at[there, rows],
            lsend_sem.at[slot, piece],
            lrecv_sem.at[there, piece],
            down,
        )

    def short_copy(slot, piece, source=None):
        rows = piece_rows(piece)
        there = slot - 4 * at_end
        drops = at_end * (1 - lax.div(slot, 8))
        return remote(
            xshort.at[slot, rows] if source is None else source.at[rows],
            xshort.at[there, rows],
            ssend_sem.at[slot, piece],
            srecv_sem.at[there, piece],
            (down_blk + drops * (drop_blk - down_blk), down_rep),
        )

    def give_copy(step, piece):
        rows = piece_rows(piece)
        there = 3 - at + step
        return remote(
            xlong.at[8 + at - step, rows],
            xshort.at[8 + there, rows],
            give_sem.at[step - 1, piece],
            take_sem.at[there, piece],
            sibling,
        )

    def give_far(slot, piece):
        rows = piece_rows(piece)
        return remote(
            xshort.at[slot, rows],
            xlong.at[3 - slot, rows],
            far_give_sem.at[slot, piece],
            lrecv_sem.at[3 - slot, piece],
            sibling,
        )

    for piece in range(PIECES):
        cross_copy(piece).start()
        short_copy(8 + at, piece, x_ref).start()

    def long_arrived(slot, piece):
        rows = piece_rows(piece)
        remote(
            xlong.at[slot, rows],
            xlong.at[slot, rows],
            lsend_sem.at[slot, piece],
            lrecv_sem.at[slot, piece],
            down,
        ).wait_recv()

    def poll_long(step, only=None):
        slot = 8 + at - step

        def one(piece, carry):
            long_arrived(slot, piece)
            if step < LONG_STEPS:
                long_copy(slot, piece).start()
            if step < REPS:

                @pl.when(at >= step)
                def _():
                    give_copy(step, piece).start()

            return carry

        if only is None:
            lax.fori_loop(0, PIECES, one, 0)
        else:
            one(only, 0)

    def poll_short(step, only=None):
        slot = 8 + at - step

        def one(piece, carry):
            rows = piece_rows(piece)
            remote(
                xshort.at[slot, rows],
                xshort.at[slot, rows],
                ssend_sem.at[slot, piece],
                srecv_sem.at[slot, piece],
                down,
            ).wait_recv()
            if step < SHORT_STEPS:
                short_copy(slot, piece).start()
            if step > REPS:

                @pl.when(slot < REPS)
                def _():
                    give_far(slot, piece).start()

            return carry

        if only is None:
            lax.fori_loop(0, PIECES, one, 0)
        else:
            one(only, 0)

    def poll_far(piece):
        for slot in range(REPS - 1):

            @pl.when(slot < at)
            def _():
                long_arrived(slot, piece)

    def project(chain, run, place, strip, with_query=False):
        rows = pl.ds(strip * STRIP, STRIP)
        shards = [chain[4 * run + i + core * (3 - 2 * i), rows] for i in range(REPS)]
        squares = jnp.zeros((STRIP, LANES), f32)
        for shard in shards:
            wide = shard.astype(f32)
            squares += wide * wide
        mean = jnp.sum(squares, axis=1, keepdims=True) * (1.0 / (REPS * LANES))
        whole = jnp.concatenate(shards, axis=1)
        parts = [wbuf[1], wbuf[2]] + ([wbuf[0]] if with_query else [])
        weights = jnp.concatenate(parts, axis=1)
        product = jnp.dot(whole, weights, preferred_element_type=f32)
        product = product * lax.rsqrt(mean + 1e-06)
        count = STRIP // BLOCK
        blocks = pl.ds(strip * count, count)
        for which in range(2):
            piece = product[:, which * LANES : (which + 1) * LANES]
            kv[place, which, blocks] = piece.astype(bf16).reshape(count, BLOCK, LANES)
        if with_query:
            piece = product[:, 2 * LANES :] * HEAD_DIM ** (-0.5)
            qbuf[blocks] = piece.astype(bf16).reshape(count, BLOCK, LANES)

    def kv_copy(index):
        place = 3 - sign * index
        there = place - sign
        return remote(
            kv.at[place], kv.at[there], ksend_sem.at[index], krecv_sem.at[index], sibling
        )

    def wo_copy():
        return remote(wobuf, owobuf, wo_sem.at[0], wo_sem.at[1], mate)

    def ready():
        for load in loads:
            load.wait()

        @pl.when(inner == 0)
        def _():
            wo_copy().start()

        for there in range(1, REPS):

            def one(piece, carry):
                @pl.when(there > at)
                def _():
                    rows = piece_rows(piece)
                    remote(
                        xlong.at[0, rows],
                        xshort.at[8 + there, rows],
                        give_sem.at[0, piece],
                        take_sem.at[there, piece],
                        sibling,
                    ).wait_recv()

                return carry

            lax.fori_loop(0, PIECES, one, 0)

    work = {
        "own": (xshort, 2, 3, 0),
        "long": (xlong, 1, 3 - sign, 1),
        "short": (xshort, 1, 3 - 2 * sign, 2),
        "far": (xlong, 0, 3 - 3 * sign, None),
    }
    for kind, number, piece in SCHEDULE:
        if kind == "L":
            poll_long(number, piece)
        elif kind == "S":
            poll_short(number, piece)
        elif kind == "F":
            poll_far(piece)
        elif kind == "ready":
            ready()
        else:
            chain, run, place, index = work[kind]
            project(chain, run, place, number, kind == "own")
            if number == STRIPS - 1 and index is not None:
                kv_copy(index).start()

    for index in range(3):
        kv_copy(index).wait_recv()

    def attend(index):
        query = qbuf[index]
        lane = lax.broadcasted_iota(jnp.int32, (BLOCK, LANES), 1)
        left = lane < HEAD_DIM
        zero = jnp.zeros_like(query)
        both = jnp.concatenate(
            [jnp.where(left, query, zero), jnp.where(left, zero, query)], axis=0
        )
        used = used_ref[index]
        keys, values, counts = [], [], []
        for slot in range(KSLOTS):
            key = key_ref[index, slot]
            place = lax.rem(lax.div(key, BLK_DEV) - blk + 3 + n_blk, n_blk) & 7
            inside = lax.rem(key, BLK_DEV)
            keys.append(kv[place, 0, inside])
            values.append(kv[place, 1, inside])
            counts.append(jnp.where(slot < used, node_ref[key], 0))
        row_lane = lax.broadcasted_iota(jnp.int32, (1, LANES), 1)
        bias = []
        for pair in range(KSLOTS // 2):
            limit = jnp.where(row_lane < BLOCK, counts[2 * pair], counts[2 * pair + 1] + BLOCK)
            bias.append(jnp.where(row_lane < limit, 0.0, NEG))
        bias = jnp.concatenate(bias, axis=1)
        scores = lax.dot_general(
            both,
            jnp.concatenate(keys, axis=0),
            (((1,), (1,)), ((), ())),
            preferred_element_type=jnp.float32,
        )
        scores = scores + bias
        top = jnp.max(scores, axis=1, keepdims=True)
        expo = jnp.exp(scores - top)
        total = jnp.sum(expo, axis=1, keepdims=True)
        mixed = jnp.dot(
            expo.astype(jnp.bfloat16),
            jnp.concatenate(values, axis=0),
            preferred_element_type=jnp.float32,
        )
        mixed = mixed / total
        att[pl.ds(index * BLOCK, BLOCK), :] = jnp.where(
            left, mixed[:BLOCK], mixed[BLOCK:]
        ).astype(jnp.bfloat16)

    def part_rows(part):
        return pl.ds(part * PART_ROWS, PART_ROWS)

    def att_copy(part):
        rows = part_rows(part)
        return remote(att.at[rows], oatt.at[rows], att_sem.at[0, part], att_sem.at[1, part], mate)

    def u_copy(part):
        return remote(usend.at[part], urecv.at[part], u_sem.at[0, part], u_sem.at[1, part], mate)

    def far_copy(part):
        return remote(
            tsend.at[part, 0], frecv.at[part], f_sem.at[0, part], f_sem.at[1, part], far
        )

    def peer_copy(part):
        return remote(
            tsend.at[part, 1], trecv.at[part], t_sem.at[0, part], t_sem.at[1, part], peer
        )

    def two_rows(part):
        rows = part_rows(part)
        return jnp.concatenate([att[rows], oatt[rows]], axis=1)

    def two_weights(column):
        return jnp.concatenate([wobuf[column], owobuf[column]], axis=0)

    def send_terms(part):
        att_copy(part).wait_recv()
        held = two_rows(part)
        for which, column, copy in ((0, far_rep, far_copy), (1, peer_rep, peer_copy)):
            term = jnp.dot(held, two_weights(column), preferred_element_type=f32)
            tsend[part, which] = term.astype(bf16)
            copy(part).start()

    @pl.when(inner == 1)
    def _():
        wo_copy().wait_recv()

    def attention_part(part, carry):
        for index in range(PART_BLOCKS):
            attend(part * PART_BLOCKS + index)

        @pl.when(inner == 0)
        def _():
            att_copy(part).start()

        @pl.when(inner == 1)
        def _():
            term = jnp.dot(att[part_rows(part)], wobuf[mate_rep], preferred_element_type=f32)
            usend[part] = term.astype(bf16)
            u_copy(part).start()

        return carry

    lax.fori_loop(0, PARTS, attention_part, 0)

    def drain(piece, carry):
        cross_copy(piece).wait_send()
        for step in range(1, LONG_STEPS):
            long_copy(8 + at - step, piece).wait_send()
        for step in range(SHORT_STEPS):
            short_copy(8 + at - step, piece).wait_send()
        for step in range(1, REPS):

            @pl.when(at >= step)
            def _():
                give_copy(step, piece).wait_send()

            @pl.when(at < step)
            def _():
                give_far(step, piece).wait_send()

        return carry

    def settle():
        for index in range(3):
            kv_copy(index).wait_send()
        lax.fori_loop(0, PIECES, drain, 0)

    def residual(part):
        return xshort[8 + at, part_rows(part)].astype(f32)

    @pl.when(inner == 1)
    def _():
        for part in range(PARTS):
            send_terms(part)
        settle()

        def finish(part, carry):
            mine = jnp.dot(two_rows(part), two_weights(rep), preferred_element_type=f32)
            mine = mine + residual(part)
            peer_copy(part).wait_recv()
            out_ref[part_rows(part), :] = (mine + trecv[part].astype(f32)).astype(bf16)
            return carry

        lax.fori_loop(0, PARTS, finish, 0)
        for part in range(PARTS):
            u_copy(part).wait_send()
            far_copy(part).wait_send()
            peer_copy(part).wait_send()

    @pl.when(inner == 0)
    def _():
        settle()

        def finish(part, carry):
            mine = jnp.dot(att[part_rows(part)], wobuf[rep], preferred_element_type=f32)
            mine = mine + residual(part)
            u_copy(part).wait_recv()
            mine = mine + urecv[part].astype(f32)
            far_copy(part).wait_recv()
            out_ref[part_rows(part), :] = (mine + frecv[part].astype(f32)).astype(bf16)
            return carry

        lax.fori_loop(0, PARTS, finish, 0)
        for part in range(PARTS):
            att_copy(part).wait_send()
        wo_copy().wait_send()


def body(x_nodes, w_qkv, w_out, pair_key, pair_count, node_count):
    n_blk = lax.axis_size("blk")
    weights = jnp.transpose(w_qkv, (1, 0, 2))
    vmem = pltpu.VMEM
    dma = pltpu.SemaphoreType.DMA
    return pl.pallas_call(
        functools.partial(kernel, n_blk),
        out_shape=pltpu.VMEM((ROWS, LANES), bf16),
        in_specs=[pl.BlockSpec(memory_space=pltpu.HBM)] * 6,
        out_specs=pl.BlockSpec(memory_space=pltpu.VMEM),
        scratch_shapes=[
            vmem((SLOTS, ROWS, LANES), bf16),
            vmem((SLOTS, ROWS, LANES), bf16),
            vmem((8, 2, BLK_DEV, BLOCK, LANES), bf16),
            vmem((BLK_DEV, BLOCK, LANES), bf16),
            vmem((3, REPS * LANES, LANES), bf16),
            vmem((REPS, LANES, LANES), bf16),
            vmem((REPS, LANES, LANES), bf16),
            vmem((ROWS, LANES), bf16),
            vmem((ROWS, LANES), bf16),
            vmem((PARTS, 2, PART_ROWS, LANES), bf16),
            vmem((PARTS, PART_ROWS, LANES), bf16),
            vmem((PARTS, PART_ROWS, LANES), bf16),
            vmem((PARTS, PART_ROWS, LANES), bf16),
            vmem((PARTS, PART_ROWS, LANES), bf16),
            pltpu.SMEM(pair_key.shape, jnp.int32),
            pltpu.SMEM(pair_count.shape, jnp.int32),
            pltpu.SMEM(node_count.shape, jnp.int32),
            dma((5 + REPS,)),
            dma((PIECES,)),
            dma((SLOTS, PIECES)),
            dma((SLOTS, PIECES)),
            dma((SLOTS, PIECES)),
            dma((SLOTS, PIECES)),
            dma((3, PIECES)),
            dma((REPS, PIECES)),
            dma((REPS, PIECES)),
            dma((3,)),
            dma((3,)),
            dma((2,)),
            dma((2, PARTS)),
            dma((2, PARTS)),
            dma((2, PARTS)),
            dma((2, PARTS)),
        ],
        compiler_params=pltpu.CompilerParams(
            collective_id=0, has_side_effects=True, vmem_limit_bytes=60 << 20
        ),
        name="graph_layer",
    )(x_nodes, weights, w_out, pair_key, pair_count, node_count)


def solution(mesh):
    return jax.shard_map(
        body,
        mesh=mesh,
        in_specs=(
            P("blk", "rep"),
            P(None, None, "rep"),
            P("rep", None),
            P("blk", None),
            P("blk"),
            P(),
        ),
        out_specs=P("blk", "rep"),
        check_vma=False,
    )
```

```python
import functools

import jax
import jax.numpy as jnp
from jax import lax
from jax.experimental import pallas as pl
from jax.experimental.pallas import tpu as pltpu
from jax.sharding import PartitionSpec as P

HEAD_DIM = 64
BLOCK = 64
KSLOTS = 8
LANES = 128
REPS = 4
ROWS = 512
BLK_DEV = 8
SLOTS = 12
LONG_STEPS = 8
SHORT_STEPS = 7
PIECES = 4
PIECE_ROWS = ROWS // PIECES
PART_ENDS = [1, 3, 5, 8]
PARTS = len(PART_ENDS)
PART_STARTS = [0] + PART_ENDS[:-1]
STRIP = 128
STRIPS = ROWS // STRIP
ORDER = [
    "L1", "S1", "L2", "S2", "L3", "S3", "L4", "ready", "own0", "S4", "own1", "L5", "own2", "S5",
    "own3", "L6", "S6", "share", "L7", "long0", "long1", "S7", "long2", "long3", "short0", "short1",
    "short2", "short3", "L8.0", "F.0", "far0", "L8.1", "F.1", "far1", "L8.2", "F.2", "far2",
    "L8.3", "F.3", "far3",
]


def parsed(words):
    found = []
    for word in words:
        kind = word.rstrip("0123456789.")
        number, _, piece = word[len(kind) :].partition(".")
        found.append((kind, int(number or 0), int(piece) if piece else None))
    return found


SCHEDULE = parsed(ORDER)
NEG = -1e30
MESH = pl.DeviceIdType.MESH
bf16 = jnp.bfloat16
f32 = jnp.float32


def kernel(
    n_blk,
    x_ref,
    w_ref,
    wo_ref,
    key_hbm,
    used_hbm,
    node_hbm,
    out_ref,
    xlong,
    xshort,
    kv,
    qbuf,
    wbuf,
    wobuf,
    owobuf,
    att,
    oatt,
    tsend,
    trecv,
    usend,
    urecv,
    frecv,
    key_ref,
    used_ref,
    node_ref,
    local_sem,
    cross_sem,
    lsend_sem,
    ssend_sem,
    lrecv_sem,
    srecv_sem,
    give_sem,
    far_give_sem,
    take_sem,
    ksend_sem,
    krecv_sem,
    wo_sem,
    att_sem,
    t_sem,
    f_sem,
    u_sem,
):
    blk = lax.axis_index("blk")
    rep = lax.axis_index("rep")
    core = lax.rem(blk, 2)
    at = rep + core * (3 - 2 * rep)
    at_end = lax.div(at, 3)
    at_start = lax.div(3 - at, 3)
    sign = 1 - 2 * core
    down_blk = lax.rem(blk + n_blk + 2 * sign * at_end, n_blk)
    up_blk = lax.rem(blk + n_blk - 2 * sign * at_start, n_blk)
    down_rep = lax.rem(rep + REPS + sign, REPS)
    up_rep = lax.rem(rep + REPS - sign, REPS)
    down = (down_blk, down_rep)
    up = (up_blk, up_rep)
    cross = (up_blk + sign, up_rep)
    sibling = (blk + sign, rep)
    inner = lax.rem(lax.div(rep + 1, 2), 2)
    mate_rep = rep + 1 - 2 * lax.rem(rep, 2)
    peer_rep = 3 - rep
    far_rep = lax.rem(rep + 2, REPS)
    drop_blk = lax.rem(blk + 6 * n_blk - 6 * sign * (at_end - at_start), n_blk)
    ends = at_end + at_start
    mate = (blk, mate_rep)
    peer = (blk, peer_rep)
    far = (blk, far_rep)

    barrier = pltpu.get_barrier_semaphore()
    for other in (down, up, cross, sibling, far):
        pl.semaphore_signal(barrier, inc=1, device_id=other, device_id_type=MESH)

    @pl.when(ends == 1)
    def _():
        pl.semaphore_signal(
            barrier,
            inc=1,
            device_id=(drop_blk, at_end * down_rep + at_start * up_rep),
            device_id_type=MESH,
        )

    loads = [
        pltpu.make_async_copy(x_ref, xshort.at[8 + at], local_sem.at[0]),
        pltpu.make_async_copy(w_ref, wbuf, local_sem.at[1]),
        pltpu.make_async_copy(key_hbm, key_ref, local_sem.at[2]),
        pltpu.make_async_copy(used_hbm, used_ref, local_sem.at[3]),
        pltpu.make_async_copy(node_hbm, node_ref, local_sem.at[4]),
    ] + [
        pltpu.make_async_copy(
            wo_ref.at[:, pl.ds(LANES * d, LANES)], wobuf.at[d], local_sem.at[5 + d]
        )
        for d in range(REPS)
    ]
    for load in loads:
        load.start()
    pl.semaphore_wait(barrier, 5 + ends)

    def remote(source, target, send_sem, recv_sem, device):
        return pltpu.make_async_remote_copy(
            src_ref=source,
            dst_ref=target,
            send_sem=send_sem,
            recv_sem=recv_sem,
            device_id=device,
            device_id_type=MESH,
        )

    def piece_rows(piece):
        return pl.ds(piece * PIECE_ROWS, PIECE_ROWS)

    def cross_copy(piece):
        slot = 11 - at - 4 * at_start
        rows = piece_rows(piece)
        return remote(
            x_ref.at[rows],
            xlong.at[slot, rows],
            cross_sem.at[piece],
            lrecv_sem.at[slot, piece],
            cross,
        )

    def long_copy(slot, piece):
        rows = piece_rows(piece)
        there = slot - 4 * at_end
        return remote(
            xlong.at[slot, rows],
            xlong.at[there, rows],
            lsend_sem.at[slot, piece],
            lrecv_sem.at[there, piece],
            down,
        )

    def short_copy(slot, piece, source=None):
        rows = piece_rows(piece)
        there = slot - 4 * at_end
        drops = at_end * (1 - lax.div(slot, 8))
        return remote(
            xshort.at[slot, rows] if source is None else source.at[rows],
            xshort.at[there, rows],
            ssend_sem.at[slot, piece],
            srecv_sem.at[there, piece],
            (down_blk + drops * (drop_blk - down_blk), down_rep),
        )

    def give_copy(step, piece):
        rows = piece_rows(piece)
        there = 3 - at + step
        return remote(
            xlong.at[8 + at - step, rows],
            xshort.at[8 + there, rows],
            give_sem.at[step - 1, piece],
            take_sem.at[there, piece],
            sibling,
        )

    def give_far(slot, piece):
        rows = piece_rows(piece)
        return remote(
            xshort.at[slot, rows],
            xlong.at[3 - slot, rows],
            far_give_sem.at[slot, piece],
            lrecv_sem.at[3 - slot, piece],
            sibling,
        )

    for piece in range(PIECES):
        cross_copy(piece).start()
        short_copy(8 + at, piece, x_ref).start()

    def long_arrived(slot, piece):
        rows = piece_rows(piece)
        remote(
            xlong.at[slot, rows],
            xlong.at[slot, rows],
            lsend_sem.at[slot, piece],
            lrecv_sem.at[slot, piece],
            down,
        ).wait_recv()

    def poll_long(step, only=None):
        slot = 8 + at - step

        def one(piece, carry):
            long_arrived(slot, piece)
            if step < LONG_STEPS:
                long_copy(slot, piece).start()
            if step < REPS:

                @pl.when(at >= step)
                def _():
                    give_copy(step, piece).start()

            return carry

        if only is None:
            lax.fori_loop(0, PIECES, one, 0)
        else:
            one(only, 0)

    def poll_short(step, only=None):
        slot = 8 + at - step

        def one(piece, carry):
            rows = piece_rows(piece)
            remote(
                xshort.at[slot, rows],
                xshort.at[slot, rows],
                ssend_sem.at[slot, piece],
                srecv_sem.at[slot, piece],
                down,
            ).wait_recv()
            if step < SHORT_STEPS:
                short_copy(slot, piece).start()
            if step > REPS:

                @pl.when(slot < REPS)
                def _():
                    give_far(slot, piece).start()

            return carry

        if only is None:
            lax.fori_loop(0, PIECES, one, 0)
        else:
            one(only, 0)

    def poll_far(piece):
        for slot in range(REPS - 1):

            @pl.when(slot < at)
            def _():
                long_arrived(slot, piece)

    def project(chain, run, place, strip, with_query=False):
        rows = pl.ds(strip * STRIP, STRIP)
        shards = [chain[4 * run + i + core * (3 - 2 * i), rows] for i in range(REPS)]
        squares = jnp.zeros((STRIP, LANES), f32)
        for shard in shards:
            wide = shard.astype(f32)
            squares += wide * wide
        mean = jnp.sum(squares, axis=1, keepdims=True) * (1.0 / (REPS * LANES))
        whole = jnp.concatenate(shards, axis=1)
        parts = [wbuf[1], wbuf[2]] + ([wbuf[0]] if with_query else [])
        weights = jnp.concatenate(parts, axis=1)
        product = jnp.dot(whole, weights, preferred_element_type=f32)
        product = product * lax.rsqrt(mean + 1e-06)
        count = STRIP // BLOCK
        blocks = pl.ds(strip * count, count)
        for which in range(2):
            piece = product[:, which * LANES : (which + 1) * LANES]
            kv[place, which, blocks] = piece.astype(bf16).reshape(count, BLOCK, LANES)
        if with_query:
            piece = product[:, 2 * LANES :] * HEAD_DIM ** (-0.5)
            qbuf[blocks] = piece.astype(bf16).reshape(count, BLOCK, LANES)

    def kv_copy(index):
        place = 3 - sign * index
        there = place - sign
        return remote(
            kv.at[place], kv.at[there], ksend_sem.at[index], krecv_sem.at[index], sibling
        )

    def wo_rows(column):
        return column, pl.ds(core * (LANES // 2), LANES // 2)

    def wo_copy(turn):
        where = wo_rows(lax.rem(rep + turn, REPS))
        return remote(
            wobuf.at[where],
            owobuf.at[where],
            wo_sem.at[0, turn - 1],
            wo_sem.at[1, turn - 1],
            mate,
        )

    def wo_share(turn):
        where = wo_rows(lax.rem(mate_rep + turn, REPS))
        return remote(
            owobuf.at[where],
            owobuf.at[where],
            wo_sem.at[2, turn - 1],
            wo_sem.at[3, turn - 1],
            sibling,
        )

    def share_weights():
        @pl.when(inner == 1)
        def _():
            for turn in range(1, REPS):
                wo_copy(turn).wait_recv()
                wo_share(turn).start()

    def ready():
        for load in loads:
            load.wait()

        @pl.when(inner == 0)
        def _():
            for turn in range(1, REPS):
                wo_copy(turn).start()

        for there in range(1, REPS):

            def one(piece, carry):
                @pl.when(there > at)
                def _():
                    rows = piece_rows(piece)
                    remote(
                        xlong.at[0, rows],
                        xshort.at[8 + there, rows],
                        give_sem.at[0, piece],
                        take_sem.at[there, piece],
                        sibling,
                    ).wait_recv()

                return carry

            lax.fori_loop(0, PIECES, one, 0)

    work = {
        "own": (xshort, 2, 3, 0),
        "long": (xlong, 1, 3 - sign, 1),
        "short": (xshort, 1, 3 - 2 * sign, 2),
        "far": (xlong, 0, 3 - 3 * sign, None),
    }
    for kind, number, piece in SCHEDULE:
        if kind == "L":
            poll_long(number, piece)
        elif kind == "S":
            poll_short(number, piece)
        elif kind == "F":
            poll_far(piece)
        elif kind == "ready":
            ready()
        elif kind == "share":
            share_weights()
        else:
            chain, run, place, index = work[kind]
            project(chain, run, place, number, kind == "own")
            if number == STRIPS - 1 and index is not None:
                kv_copy(index).start()

    for index in range(3):
        kv_copy(index).wait_recv()

    def attend(index):
        query = qbuf[index]
        lane = lax.broadcasted_iota(jnp.int32, (BLOCK, LANES), 1)
        left = lane < HEAD_DIM
        zero = jnp.zeros_like(query)
        both = jnp.concatenate(
            [jnp.where(left, query, zero), jnp.where(left, zero, query)], axis=0
        )
        used = used_ref[index]
        keys, values, counts = [], [], []
        for slot in range(KSLOTS):
            key = key_ref[index, slot]
            place = lax.rem(lax.div(key, BLK_DEV) - blk + 3 + n_blk, n_blk) & 7
            inside = lax.rem(key, BLK_DEV)
            keys.append(kv[place, 0, inside])
            values.append(kv[place, 1, inside])
            counts.append(jnp.where(slot < used, node_ref[key], 0))
        row_lane = lax.broadcasted_iota(jnp.int32, (1, LANES), 1)
        bias = []
        for pair in range(KSLOTS // 2):
            limit = jnp.where(row_lane < BLOCK, counts[2 * pair], counts[2 * pair + 1] + BLOCK)
            bias.append(jnp.where(row_lane < limit, 0.0, NEG))
        bias = jnp.concatenate(bias, axis=1)
        scores = lax.dot_general(
            both,
            jnp.concatenate(keys, axis=0),
            (((1,), (1,)), ((), ())),
            preferred_element_type=jnp.float32,
        )
        scores = scores + bias
        top = jnp.max(scores, axis=1, keepdims=True)
        expo = jnp.exp(scores - top)
        total = jnp.sum(expo, axis=1, keepdims=True)
        mixed = jnp.dot(
            expo.astype(jnp.bfloat16),
            jnp.concatenate(values, axis=0),
            preferred_element_type=jnp.float32,
        )
        mixed = mixed / total
        att[pl.ds(index * BLOCK, BLOCK), :] = jnp.where(
            left, mixed[:BLOCK], mixed[BLOCK:]
        ).astype(jnp.bfloat16)

    def part_rows(part):
        count = PART_ENDS[part] - PART_STARTS[part]
        return pl.ds(PART_STARTS[part] * BLOCK, count * BLOCK)

    def att_copy(part):
        rows = part_rows(part)
        return remote(att.at[rows], oatt.at[rows], att_sem.at[0, part], att_sem.at[1, part], mate)

    def u_copy(part):
        rows = part_rows(part)
        return remote(usend.at[rows], urecv.at[rows], u_sem.at[0, part], u_sem.at[1, part], mate)

    def far_copy(part):
        rows = part_rows(part)
        return remote(
            tsend.at[0, rows], frecv.at[rows], f_sem.at[0, part], f_sem.at[1, part], far
        )

    def peer_copy(part):
        rows = part_rows(part)
        return remote(
            tsend.at[1, rows], trecv.at[rows], t_sem.at[0, part], t_sem.at[1, part], peer
        )

    def two_rows(part):
        rows = part_rows(part)
        return jnp.concatenate([att[rows, :], oatt[rows, :]], axis=1)

    def two_weights(column):
        return jnp.concatenate([wobuf[column], owobuf[column]], axis=0)

    def send_terms(part):
        att_copy(part).wait_recv()
        held = two_rows(part)
        for which, column, copy in ((0, far_rep, far_copy), (1, peer_rep, peer_copy)):
            term = jnp.dot(held, two_weights(column), preferred_element_type=f32)
            tsend[which, part_rows(part), :] = term.astype(bf16)
            copy(part).start()

    @pl.when(inner == 1)
    def _():
        for turn in range(1, REPS):
            wo_share(turn).wait_recv()

    for part in range(PARTS):
        for index in range(PART_STARTS[part], PART_ENDS[part]):
            attend(index)

        @pl.when(inner == 0)
        def _():
            att_copy(part).start()

        @pl.when(inner == 1)
        def _():
            rows = part_rows(part)
            term = jnp.dot(att[rows, :], wobuf[mate_rep], preferred_element_type=f32)
            usend[rows, :] = term.astype(bf16)
            u_copy(part).start()

    def drain(piece, carry):
        cross_copy(piece).wait_send()
        for step in range(1, LONG_STEPS):
            long_copy(8 + at - step, piece).wait_send()
        for step in range(SHORT_STEPS):
            short_copy(8 + at - step, piece).wait_send()
        for step in range(1, REPS):

            @pl.when(at >= step)
            def _():
                give_copy(step, piece).wait_send()

            @pl.when(at < step)
            def _():
                give_far(step, piece).wait_send()

        return carry

    def settle():
        for index in range(3):
            kv_copy(index).wait_send()
        lax.fori_loop(0, PIECES, drain, 0)

    def residual(part):
        return xshort[8 + at, part_rows(part), :].astype(f32)

    @pl.when(inner == 1)
    def _():
        for part in range(PARTS):
            send_terms(part)
        settle()

        for part in range(PARTS):
            rows = part_rows(part)
            mine = jnp.dot(two_rows(part), two_weights(rep), preferred_element_type=f32)
            mine = mine + residual(part)
            peer_copy(part).wait_recv()
            out_ref[rows, :] = (mine + trecv[rows, :].astype(f32)).astype(bf16)
        for part in range(PARTS):
            u_copy(part).wait_send()
            far_copy(part).wait_send()
            peer_copy(part).wait_send()
        for turn in range(1, REPS):
            wo_share(turn).wait_send()

    @pl.when(inner == 0)
    def _():
        settle()

        for part in range(PARTS):
            rows = part_rows(part)
            mine = jnp.dot(att[rows, :], wobuf[rep], preferred_element_type=f32)
            mine = mine + residual(part)
            u_copy(part).wait_recv()
            mine = mine + urecv[rows, :].astype(f32)
            far_copy(part).wait_recv()
            out_ref[rows, :] = (mine + frecv[rows, :].astype(f32)).astype(bf16)
        for part in range(PARTS):
            att_copy(part).wait_send()
        for turn in range(1, REPS):
            wo_copy(turn).wait_send()


def body(x_nodes, w_qkv, w_out, pair_key, pair_count, node_count):
    n_blk = lax.axis_size("blk")
    weights = jnp.transpose(w_qkv, (1, 0, 2))
    vmem = pltpu.VMEM
    dma = pltpu.SemaphoreType.DMA
    return pl.pallas_call(
        functools.partial(kernel, n_blk),
        out_shape=pltpu.VMEM((ROWS, LANES), bf16),
        in_specs=[pl.BlockSpec(memory_space=pltpu.HBM)] * 6,
        out_specs=pl.BlockSpec(memory_space=pltpu.VMEM),
        scratch_shapes=[
            vmem((SLOTS, ROWS, LANES), bf16),
            vmem((SLOTS, ROWS, LANES), bf16),
            vmem((8, 2, BLK_DEV, BLOCK, LANES), bf16),
            vmem((BLK_DEV, BLOCK, LANES), bf16),
            vmem((3, REPS * LANES, LANES), bf16),
            vmem((REPS, LANES, LANES), bf16),
            vmem((REPS, LANES, LANES), bf16),
            vmem((ROWS, LANES), bf16),
            vmem((ROWS, LANES), bf16),
            vmem((2, ROWS, LANES), bf16),
            vmem((ROWS, LANES), bf16),
            vmem((ROWS, LANES), bf16),
            vmem((ROWS, LANES), bf16),
            vmem((ROWS, LANES), bf16),
            pltpu.SMEM(pair_key.shape, jnp.int32),
            pltpu.SMEM(pair_count.shape, jnp.int32),
            pltpu.SMEM(node_count.shape, jnp.int32),
            dma((5 + REPS,)),
            dma((PIECES,)),
            dma((SLOTS, PIECES)),
            dma((SLOTS, PIECES)),
            dma((SLOTS, PIECES)),
            dma((SLOTS, PIECES)),
            dma((3, PIECES)),
            dma((REPS, PIECES)),
            dma((REPS, PIECES)),
            dma((3,)),
            dma((3,)),
            dma((4, REPS - 1)),
            dma((2, PARTS)),
            dma((2, PARTS)),
            dma((2, PARTS)),
            dma((2, PARTS)),
        ],
        compiler_params=pltpu.CompilerParams(
            collective_id=0, has_side_effects=True, vmem_limit_bytes=60 << 20
        ),
        name="graph_layer",
    )(x_nodes, weights, w_out, pair_key, pair_count, node_count)


def solution(mesh):
    return jax.shard_map(
        body,
        mesh=mesh,
        in_specs=(
            P("blk", "rep"),
            P(None, None, "rep"),
            P("rep", None),
            P("blk", None),
            P("blk"),
            P(),
        ),
        out_specs=P("blk", "rep"),
        check_vma=False,
    )
```

```python
import functools

import jax
import jax.numpy as jnp
from jax import lax
from jax.experimental import pallas as pl
from jax.experimental.pallas import tpu as pltpu
from jax.sharding import PartitionSpec as P

HEAD_DIM = 64
BLOCK = 64
KSLOTS = 8
LANES = 128
REPS = 4
ROWS = 512
BLK_DEV = 8
SLOTS = 12
LONG_STEPS = 8
SHORT_STEPS = 7
PIECES = 4
PIECE_ROWS = ROWS // PIECES
PART_ENDS = [2, 5, 8]
PARTS = len(PART_ENDS)
PART_STARTS = [0] + PART_ENDS[:-1]
STRIP = 128
STRIPS = ROWS // STRIP
ORDER = [
    "B1", "B2", "B3", "B4", "ready", "own0", "own1", "B5", "own2", "own3", "B6", "share", "B7",
    "long0", "long1", "long2", "long3", "short0", "short1", "short2", "short3", "L8.0", "F.0",
    "far0", "L8.1", "F.1", "far1", "L8.2", "F.2", "far2", "L8.3", "F.3", "far3",
]


def parsed(words):
    found = []
    for word in words:
        kind = word.rstrip("0123456789.")
        number, _, piece = word[len(kind) :].partition(".")
        found.append((kind, int(number or 0), int(piece) if piece else None))
    return found


SCHEDULE = parsed(ORDER)
NEG = -1e30
MESH = pl.DeviceIdType.MESH
bf16 = jnp.bfloat16
f32 = jnp.float32


def kernel(
    n_blk,
    x_ref,
    w_ref,
    wo_ref,
    key_hbm,
    used_hbm,
    node_hbm,
    out_ref,
    xlong,
    xshort,
    kv,
    qbuf,
    wbuf,
    wobuf,
    owobuf,
    att,
    oatt,
    tsend,
    trecv,
    usend,
    urecv,
    frecv,
    key_ref,
    used_ref,
    node_ref,
    local_sem,
    cross_sem,
    lsend_sem,
    ssend_sem,
    lrecv_sem,
    srecv_sem,
    give_sem,
    far_give_sem,
    take_sem,
    ksend_sem,
    krecv_sem,
    wo_sem,
    att_sem,
    t_sem,
    f_sem,
    u_sem,
):
    blk = lax.axis_index("blk")
    rep = lax.axis_index("rep")
    core = lax.rem(blk, 2)
    at = rep + core * (3 - 2 * rep)
    at_end = lax.div(at, 3)
    at_start = lax.div(3 - at, 3)
    sign = 1 - 2 * core
    down_blk = lax.rem(blk + n_blk + 2 * sign * at_end, n_blk)
    up_blk = lax.rem(blk + n_blk - 2 * sign * at_start, n_blk)
    down_rep = lax.rem(rep + REPS + sign, REPS)
    up_rep = lax.rem(rep + REPS - sign, REPS)
    down = (down_blk, down_rep)
    up = (up_blk, up_rep)
    cross = (up_blk + sign, up_rep)
    sibling = (blk + sign, rep)
    inner = lax.rem(lax.div(rep + 1, 2), 2)
    mate_rep = rep + 1 - 2 * lax.rem(rep, 2)
    peer_rep = 3 - rep
    far_rep = lax.rem(rep + 2, REPS)
    drop_blk = lax.rem(blk + 6 * n_blk - 6 * sign * (at_end - at_start), n_blk)
    ends = at_end + at_start
    mate = (blk, mate_rep)
    peer = (blk, peer_rep)
    far = (blk, far_rep)

    barrier = pltpu.get_barrier_semaphore()
    for other in (down, up, cross, sibling, far):
        pl.semaphore_signal(barrier, inc=1, device_id=other, device_id_type=MESH)

    @pl.when(ends == 1)
    def _():
        pl.semaphore_signal(
            barrier,
            inc=1,
            device_id=(drop_blk, at_end * down_rep + at_start * up_rep),
            device_id_type=MESH,
        )

    loads = [
        pltpu.make_async_copy(x_ref, xshort.at[8 + at], local_sem.at[0]),
        pltpu.make_async_copy(w_ref, wbuf, local_sem.at[1]),
        pltpu.make_async_copy(key_hbm, key_ref, local_sem.at[2]),
        pltpu.make_async_copy(used_hbm, used_ref, local_sem.at[3]),
        pltpu.make_async_copy(node_hbm, node_ref, local_sem.at[4]),
    ] + [
        pltpu.make_async_copy(
            wo_ref.at[:, pl.ds(LANES * d, LANES)], wobuf.at[d], local_sem.at[5 + d]
        )
        for d in range(REPS)
    ]
    for load in loads:
        load.start()
    pl.semaphore_wait(barrier, 5 + ends)

    def remote(source, target, send_sem, recv_sem, device):
        return pltpu.make_async_remote_copy(
            src_ref=source,
            dst_ref=target,
            send_sem=send_sem,
            recv_sem=recv_sem,
            device_id=device,
            device_id_type=MESH,
        )

    def piece_rows(piece):
        return pl.ds(piece * PIECE_ROWS, PIECE_ROWS)

    def cross_copy(piece):
        slot = 11 - at - 4 * at_start
        rows = piece_rows(piece)
        return remote(
            x_ref.at[rows],
            xlong.at[slot, rows],
            cross_sem.at[piece],
            lrecv_sem.at[slot, piece],
            cross,
        )

    def long_copy(slot, piece):
        rows = piece_rows(piece)
        there = slot - 4 * at_end
        return remote(
            xlong.at[slot, rows],
            xlong.at[there, rows],
            lsend_sem.at[slot, piece],
            lrecv_sem.at[there, piece],
            down,
        )

    def short_copy(slot, piece, source=None):
        rows = piece_rows(piece)
        there = slot - 4 * at_end
        drops = at_end * (1 - lax.div(slot, 8))
        return remote(
            xshort.at[slot, rows] if source is None else source.at[rows],
            xshort.at[there, rows],
            ssend_sem.at[slot, piece],
            srecv_sem.at[there, piece],
            (down_blk + drops * (drop_blk - down_blk), down_rep),
        )

    def give_copy(step, piece):
        rows = piece_rows(piece)
        there = 3 - at + step
        return remote(
            xlong.at[8 + at - step, rows],
            xshort.at[8 + there, rows],
            give_sem.at[step - 1, piece],
            take_sem.at[there, piece],
            sibling,
        )

    def give_far(slot, piece):
        rows = piece_rows(piece)
        return remote(
            xshort.at[slot, rows],
            xlong.at[3 - slot, rows],
            far_give_sem.at[slot, piece],
            lrecv_sem.at[3 - slot, piece],
            sibling,
        )

    for piece in range(PIECES):
        cross_copy(piece).start()
        short_copy(8 + at, piece, x_ref).start()

    def long_arrived(slot, piece):
        rows = piece_rows(piece)
        remote(
            xlong.at[slot, rows],
            xlong.at[slot, rows],
            lsend_sem.at[slot, piece],
            lrecv_sem.at[slot, piece],
            down,
        ).wait_recv()

    def take_long(step, piece):
        slot = 8 + at - step
        long_arrived(slot, piece)
        if step < LONG_STEPS:
            long_copy(slot, piece).start()
        if step < REPS:

            @pl.when(at >= step)
            def _():
                give_copy(step, piece).start()

    def take_short(step, piece):
        slot = 8 + at - step
        rows = piece_rows(piece)
        remote(
            xshort.at[slot, rows],
            xshort.at[slot, rows],
            ssend_sem.at[slot, piece],
            srecv_sem.at[slot, piece],
            down,
        ).wait_recv()
        if step < SHORT_STEPS:
            short_copy(slot, piece).start()
        if step > REPS:

            @pl.when(slot < REPS)
            def _():
                give_far(slot, piece).start()

    def poll(chains, step, only):
        def one(piece, carry):
            for take in chains:
                take(step, piece)
            return carry

        if only is None:
            lax.fori_loop(0, PIECES, one, 0)
        else:
            one(only, 0)

    def poll_far(piece):
        for slot in range(REPS - 1):

            @pl.when(slot < at)
            def _():
                long_arrived(slot, piece)

    def project(chain, run, place, strip, with_query=False):
        rows = pl.ds(strip * STRIP, STRIP)
        shards = [chain[4 * run + i + core * (3 - 2 * i), rows] for i in range(REPS)]
        squares = jnp.zeros((STRIP, LANES), f32)
        for shard in shards:
            wide = shard.astype(f32)
            squares += wide * wide
        mean = jnp.sum(squares, axis=1, keepdims=True) * (1.0 / (REPS * LANES))
        whole = jnp.concatenate(shards, axis=1)
        parts = [wbuf[1], wbuf[2]] + ([wbuf[0]] if with_query else [])
        weights = jnp.concatenate(parts, axis=1)
        product = jnp.dot(whole, weights, preferred_element_type=f32)
        product = product * lax.rsqrt(mean + 1e-06)
        count = STRIP // BLOCK
        blocks = pl.ds(strip * count, count)
        for which in range(2):
            piece = product[:, which * LANES : (which + 1) * LANES]
            kv[place, which, blocks] = piece.astype(bf16).reshape(count, BLOCK, LANES)
        if with_query:
            piece = product[:, 2 * LANES :] * HEAD_DIM ** (-0.5)
            qbuf[blocks] = piece.astype(bf16).reshape(count, BLOCK, LANES)

    def kv_copy(index):
        place = 3 - sign * index
        there = place - sign
        return remote(
            kv.at[place], kv.at[there], ksend_sem.at[index], krecv_sem.at[index], sibling
        )

    def wo_rows(column):
        return column, pl.ds(core * (LANES // 2), LANES // 2)

    def wo_copy(turn):
        where = wo_rows(lax.rem(rep + turn, REPS))
        return remote(
            wobuf.at[where],
            owobuf.at[where],
            wo_sem.at[0, turn - 1],
            wo_sem.at[1, turn - 1],
            mate,
        )

    def wo_share(turn):
        where = wo_rows(lax.rem(mate_rep + turn, REPS))
        return remote(
            owobuf.at[where],
            owobuf.at[where],
            wo_sem.at[2, turn - 1],
            wo_sem.at[3, turn - 1],
            sibling,
        )

    def share_weights():
        @pl.when(inner == 1)
        def _():
            for turn in range(1, REPS):
                wo_copy(turn).wait_recv()
                wo_share(turn).start()

    def ready():
        for load in loads:
            load.wait()

        @pl.when(inner == 0)
        def _():
            for turn in range(1, REPS):
                wo_copy(turn).start()

        for there in range(1, REPS):

            def one(piece, carry):
                @pl.when(there > at)
                def _():
                    rows = piece_rows(piece)
                    remote(
                        xlong.at[0, rows],
                        xshort.at[8 + there, rows],
                        give_sem.at[0, piece],
                        take_sem.at[there, piece],
                        sibling,
                    ).wait_recv()

                return carry

            lax.fori_loop(0, PIECES, one, 0)

    chains = {"L": [take_long], "S": [take_short], "B": [take_long, take_short]}
    work = {
        "own": (xshort, 2, 3, 0),
        "long": (xlong, 1, 3 - sign, 1),
        "short": (xshort, 1, 3 - 2 * sign, 2),
        "far": (xlong, 0, 3 - 3 * sign, None),
    }
    for kind, number, piece in SCHEDULE:
        if kind in chains:
            poll(chains[kind], number, piece)
        elif kind == "F":
            poll_far(piece)
        elif kind == "ready":
            ready()
        elif kind == "share":
            share_weights()
        else:
            chain, run, place, index = work[kind]
            project(chain, run, place, number, kind == "own")
            if number == STRIPS - 1 and index is not None:
                kv_copy(index).start()

    for index in range(3):
        kv_copy(index).wait_recv()

    def attend(index):
        query = qbuf[index]
        lane = lax.broadcasted_iota(jnp.int32, (BLOCK, LANES), 1)
        left = lane < HEAD_DIM
        zero = jnp.zeros_like(query)
        both = jnp.concatenate(
            [jnp.where(left, query, zero), jnp.where(left, zero, query)], axis=0
        )
        used = used_ref[index]
        keys, values, counts = [], [], []
        for slot in range(KSLOTS):
            key = key_ref[index, slot]
            place = lax.rem(lax.div(key, BLK_DEV) - blk + 3 + n_blk, n_blk) & 7
            inside = lax.rem(key, BLK_DEV)
            keys.append(kv[place, 0, inside])
            values.append(kv[place, 1, inside])
            counts.append(jnp.where(slot < used, node_ref[key], 0))
        row_lane = lax.broadcasted_iota(jnp.int32, (1, LANES), 1)
        bias = []
        for pair in range(KSLOTS // 2):
            limit = jnp.where(row_lane < BLOCK, counts[2 * pair], counts[2 * pair + 1] + BLOCK)
            bias.append(jnp.where(row_lane < limit, 0.0, NEG))
        bias = jnp.concatenate(bias, axis=1)
        scores = lax.dot_general(
            both,
            jnp.concatenate(keys, axis=0),
            (((1,), (1,)), ((), ())),
            preferred_element_type=jnp.float32,
        )
        scores = scores + bias
        top = jnp.max(scores, axis=1, keepdims=True)
        expo = jnp.exp(scores - top)
        total = jnp.sum(expo, axis=1, keepdims=True)
        mixed = jnp.dot(
            expo.astype(jnp.bfloat16),
            jnp.concatenate(values, axis=0),
            preferred_element_type=jnp.float32,
        )
        mixed = mixed / total
        att[pl.ds(index * BLOCK, BLOCK), :] = jnp.where(
            left, mixed[:BLOCK], mixed[BLOCK:]
        ).astype(jnp.bfloat16)

    def part_rows(part):
        count = PART_ENDS[part] - PART_STARTS[part]
        return pl.ds(PART_STARTS[part] * BLOCK, count * BLOCK)

    def att_copy(part):
        rows = part_rows(part)
        return remote(att.at[rows], oatt.at[rows], att_sem.at[0, part], att_sem.at[1, part], mate)

    def u_copy(part):
        rows = part_rows(part)
        return remote(usend.at[rows], urecv.at[rows], u_sem.at[0, part], u_sem.at[1, part], mate)

    def far_copy(part):
        rows = part_rows(part)
        return remote(
            tsend.at[0, rows], frecv.at[rows], f_sem.at[0, part], f_sem.at[1, part], far
        )

    def peer_copy(part):
        rows = part_rows(part)
        return remote(
            tsend.at[1, rows], trecv.at[rows], t_sem.at[0, part], t_sem.at[1, part], peer
        )

    def two_rows(part):
        rows = part_rows(part)
        return jnp.concatenate([att[rows, :], oatt[rows, :]], axis=1)

    def two_weights(column):
        return jnp.concatenate([wobuf[column], owobuf[column]], axis=0)

    def send_terms(part):
        att_copy(part).wait_recv()
        held = two_rows(part)
        columns = jnp.concatenate([two_weights(far_rep), two_weights(peer_rep)], axis=1)
        terms = jnp.dot(held, columns, preferred_element_type=f32).astype(bf16)
        for which, copy in ((0, far_copy), (1, peer_copy)):
            tsend[which, part_rows(part), :] = terms[:, which * LANES : (which + 1) * LANES]
            copy(part).start()

    @pl.when(inner == 1)
    def _():
        for turn in range(1, REPS):
            wo_share(turn).wait_recv()

    for part in range(PARTS):
        for index in range(PART_STARTS[part], PART_ENDS[part]):
            attend(index)

        @pl.when(inner == 0)
        def _():
            att_copy(part).start()

        @pl.when(inner == 1)
        def _():
            rows = part_rows(part)
            term = jnp.dot(att[rows, :], wobuf[mate_rep], preferred_element_type=f32)
            usend[rows, :] = term.astype(bf16)
            u_copy(part).start()

    def drain(piece, carry):
        cross_copy(piece).wait_send()
        for step in range(1, LONG_STEPS):
            long_copy(8 + at - step, piece).wait_send()
        for step in range(SHORT_STEPS):
            short_copy(8 + at - step, piece).wait_send()
        for step in range(1, REPS):

            @pl.when(at >= step)
            def _():
                give_copy(step, piece).wait_send()

            @pl.when(at < step)
            def _():
                give_far(step, piece).wait_send()

        return carry

    def settle():
        for index in range(3):
            kv_copy(index).wait_send()
        lax.fori_loop(0, PIECES, drain, 0)

    def residual(part):
        return xshort[8 + at, part_rows(part), :].astype(f32)

    @pl.when(inner == 1)
    def _():
        for part in range(PARTS):
            send_terms(part)
        settle()

        for part in range(PARTS):
            rows = part_rows(part)
            mine = jnp.dot(two_rows(part), two_weights(rep), preferred_element_type=f32)
            mine = mine + residual(part)
            peer_copy(part).wait_recv()
            out_ref[rows, :] = (mine + trecv[rows, :].astype(f32)).astype(bf16)
        for part in range(PARTS):
            u_copy(part).wait_send()
            far_copy(part).wait_send()
            peer_copy(part).wait_send()
        for turn in range(1, REPS):
            wo_share(turn).wait_send()

    @pl.when(inner == 0)
    def _():
        settle()

        for part in range(PARTS):
            rows = part_rows(part)
            mine = jnp.dot(att[rows, :], wobuf[rep], preferred_element_type=f32)
            mine = mine + residual(part)
            u_copy(part).wait_recv()
            mine = mine + urecv[rows, :].astype(f32)
            far_copy(part).wait_recv()
            out_ref[rows, :] = (mine + frecv[rows, :].astype(f32)).astype(bf16)
        for part in range(PARTS):
            att_copy(part).wait_send()
        for turn in range(1, REPS):
            wo_copy(turn).wait_send()


def body(x_nodes, w_qkv, w_out, pair_key, pair_count, node_count):
    n_blk = lax.axis_size("blk")
    weights = jnp.transpose(w_qkv, (1, 0, 2))
    vmem = pltpu.VMEM
    dma = pltpu.SemaphoreType.DMA
    return pl.pallas_call(
        functools.partial(kernel, n_blk),
        out_shape=pltpu.VMEM((ROWS, LANES), bf16),
        in_specs=[pl.BlockSpec(memory_space=pltpu.HBM)] * 6,
        out_specs=pl.BlockSpec(memory_space=pltpu.VMEM),
        scratch_shapes=[
            vmem((SLOTS, ROWS, LANES), bf16),
            vmem((SLOTS, ROWS, LANES), bf16),
            vmem((8, 2, BLK_DEV, BLOCK, LANES), bf16),
            vmem((BLK_DEV, BLOCK, LANES), bf16),
            vmem((3, REPS * LANES, LANES), bf16),
            vmem((REPS, LANES, LANES), bf16),
            vmem((REPS, LANES, LANES), bf16),
            vmem((ROWS, LANES), bf16),
            vmem((ROWS, LANES), bf16),
            vmem((2, ROWS, LANES), bf16),
            vmem((ROWS, LANES), bf16),
            vmem((ROWS, LANES), bf16),
            vmem((ROWS, LANES), bf16),
            vmem((ROWS, LANES), bf16),
            pltpu.SMEM(pair_key.shape, jnp.int32),
            pltpu.SMEM(pair_count.shape, jnp.int32),
            pltpu.SMEM(node_count.shape, jnp.int32),
            dma((5 + REPS,)),
            dma((PIECES,)),
            dma((SLOTS, PIECES)),
            dma((SLOTS, PIECES)),
            dma((SLOTS, PIECES)),
            dma((SLOTS, PIECES)),
            dma((3, PIECES)),
            dma((REPS, PIECES)),
            dma((REPS, PIECES)),
            dma((3,)),
            dma((3,)),
            dma((4, REPS - 1)),
            dma((2, PARTS)),
            dma((2, PARTS)),
            dma((2, PARTS)),
            dma((2, PARTS)),
        ],
        compiler_params=pltpu.CompilerParams(
            collective_id=0, has_side_effects=True, vmem_limit_bytes=60 << 20
        ),
        name="graph_layer",
    )(x_nodes, weights, w_out, pair_key, pair_count, node_count)


def solution(mesh):
    return jax.shard_map(
        body,
        mesh=mesh,
        in_specs=(
            P("blk", "rep"),
            P(None, None, "rep"),
            P("rep", None),
            P("blk", None),
            P("blk"),
            P(),
        ),
        out_specs=P("blk", "rep"),
        check_vma=False,
    )
```

```python
import functools

import jax
import jax.numpy as jnp
from jax import lax
from jax.experimental import pallas as pl
from jax.experimental.pallas import tpu as pltpu
from jax.sharding import PartitionSpec as P

HEAD_DIM = 64
BLOCK = 64
KSLOTS = 8
LANES = 128
REPS = 4
ROWS = 512
BLK_DEV = 8
SLOTS = 12
LONG_STEPS = 8
SHORT_STEPS = 7
PIECES = 4
PIECE_ROWS = ROWS // PIECES
PART_ENDS = [2, 5, 8]
PARTS = len(PART_ENDS)
PART_STARTS = [0] + PART_ENDS[:-1]
STRIP = 128
STRIPS = ROWS // STRIP
ORDER = [
    "B1", "B2", "B3", "B4", "ready", "B5.0", "own0", "B5.1", "own1", "B5.2", "own2", "B5.3",
    "own3", "B6", "share", "B7.0", "long0", "short0", "B7.1", "long1", "short1", "B7.2",
    "long2", "short2", "B7.3", "long3", "short3", "L8.0", "F.0", "far0", "L8.1", "F.1", "far1",
    "L8.2", "F.2", "far2", "L8.3", "F.3", "far3",
]


def parsed(words):
    found = []
    for word in words:
        kind = word.rstrip("0123456789.")
        number, _, piece = word[len(kind) :].partition(".")
        found.append((kind, int(number or 0), int(piece) if piece else None))
    return found


SCHEDULE = parsed(ORDER)
NEG = -1e30
MESH = pl.DeviceIdType.MESH
bf16 = jnp.bfloat16
f32 = jnp.float32


def kernel(
    n_blk,
    x_ref,
    w_ref,
    wo_ref,
    key_hbm,
    used_hbm,
    node_hbm,
    out_ref,
    xlong,
    xshort,
    kv,
    qbuf,
    wbuf,
    wobuf,
    owobuf,
    att,
    oatt,
    tsend,
    trecv,
    usend,
    urecv,
    frecv,
    key_ref,
    used_ref,
    node_ref,
    local_sem,
    cross_sem,
    lsend_sem,
    ssend_sem,
    lrecv_sem,
    srecv_sem,
    give_sem,
    far_give_sem,
    take_sem,
    ksend_sem,
    krecv_sem,
    wo_sem,
    att_sem,
    t_sem,
    f_sem,
    u_sem,
):
    blk = lax.axis_index("blk")
    rep = lax.axis_index("rep")
    core = lax.rem(blk, 2)
    at = rep + core * (3 - 2 * rep)
    at_end = lax.div(at, 3)
    at_start = lax.div(3 - at, 3)
    sign = 1 - 2 * core
    down_blk = lax.rem(blk + n_blk + 2 * sign * at_end, n_blk)
    up_blk = lax.rem(blk + n_blk - 2 * sign * at_start, n_blk)
    down_rep = lax.rem(rep + REPS + sign, REPS)
    up_rep = lax.rem(rep + REPS - sign, REPS)
    down = (down_blk, down_rep)
    up = (up_blk, up_rep)
    cross = (up_blk + sign, up_rep)
    sibling = (blk + sign, rep)
    inner = lax.rem(lax.div(rep + 1, 2), 2)
    mate_rep = rep + 1 - 2 * lax.rem(rep, 2)
    peer_rep = 3 - rep
    far_rep = lax.rem(rep + 2, REPS)
    drop_blk = lax.rem(blk + 6 * n_blk - 6 * sign * (at_end - at_start), n_blk)
    ends = at_end + at_start
    mate = (blk, mate_rep)
    peer = (blk, peer_rep)
    far = (blk, far_rep)

    barrier = pltpu.get_barrier_semaphore()
    for other in (down, up, cross, sibling, far):
        pl.semaphore_signal(barrier, inc=1, device_id=other, device_id_type=MESH)

    @pl.when(ends == 1)
    def _():
        pl.semaphore_signal(
            barrier,
            inc=1,
            device_id=(drop_blk, at_end * down_rep + at_start * up_rep),
            device_id_type=MESH,
        )

    loads = [
        pltpu.make_async_copy(x_ref, xshort.at[8 + at], local_sem.at[0]),
        pltpu.make_async_copy(w_ref, wbuf, local_sem.at[1]),
        pltpu.make_async_copy(key_hbm, key_ref, local_sem.at[2]),
        pltpu.make_async_copy(used_hbm, used_ref, local_sem.at[3]),
        pltpu.make_async_copy(node_hbm, node_ref, local_sem.at[4]),
    ] + [
        pltpu.make_async_copy(
            wo_ref.at[:, pl.ds(LANES * d, LANES)], wobuf.at[d], local_sem.at[5 + d]
        )
        for d in range(REPS)
    ]
    for load in loads:
        load.start()
    pl.semaphore_wait(barrier, 5 + ends)

    def remote(source, target, send_sem, recv_sem, device):
        return pltpu.make_async_remote_copy(
            src_ref=source,
            dst_ref=target,
            send_sem=send_sem,
            recv_sem=recv_sem,
            device_id=device,
            device_id_type=MESH,
        )

    def piece_rows(piece):
        return pl.ds(piece * PIECE_ROWS, PIECE_ROWS)

    def cross_copy(piece):
        slot = 11 - at - 4 * at_start
        rows = piece_rows(piece)
        return remote(
            x_ref.at[rows],
            xlong.at[slot, rows],
            cross_sem.at[0],
            lrecv_sem.at[slot, piece],
            cross,
        )

    def long_copy(slot, piece):
        rows = piece_rows(piece)
        there = slot - 4 * at_end
        return remote(
            xlong.at[slot, rows],
            xlong.at[there, rows],
            lsend_sem.at[slot],
            lrecv_sem.at[there, piece],
            down,
        )

    def short_copy(slot, piece, source=None):
        rows = piece_rows(piece)
        there = slot - 4 * at_end
        drops = at_end * (1 - lax.div(slot, 8))
        return remote(
            xshort.at[slot, rows] if source is None else source.at[rows],
            xshort.at[there, rows],
            ssend_sem.at[slot],
            srecv_sem.at[there, piece],
            (down_blk + drops * (drop_blk - down_blk), down_rep),
        )

    def give_copy(step, piece):
        rows = piece_rows(piece)
        there = 3 - at + step
        return remote(
            xlong.at[8 + at - step, rows],
            xshort.at[8 + there, rows],
            give_sem.at[step - 1],
            take_sem.at[there, piece],
            sibling,
        )

    def give_far(slot, piece):
        rows = piece_rows(piece)
        return remote(
            xshort.at[slot, rows],
            xlong.at[3 - slot, rows],
            far_give_sem.at[slot],
            lrecv_sem.at[3 - slot, piece],
            sibling,
        )

    for piece in range(PIECES):
        cross_copy(piece).start()
        short_copy(8 + at, piece, x_ref).start()

    def long_arrived(slot, piece):
        rows = piece_rows(piece)
        remote(
            xlong.at[slot, rows],
            xlong.at[slot, rows],
            lsend_sem.at[slot],
            lrecv_sem.at[slot, piece],
            down,
        ).wait_recv()

    def take_long(step, piece):
        slot = 8 + at - step
        long_arrived(slot, piece)
        if step < LONG_STEPS:
            long_copy(slot, piece).start()
        if step < REPS:

            @pl.when(at >= step)
            def _():
                give_copy(step, piece).start()

    def take_short(step, piece):
        slot = 8 + at - step
        rows = piece_rows(piece)
        remote(
            xshort.at[slot, rows],
            xshort.at[slot, rows],
            ssend_sem.at[slot],
            srecv_sem.at[slot, piece],
            down,
        ).wait_recv()
        if step < SHORT_STEPS:
            short_copy(slot, piece).start()
        if step > REPS:

            @pl.when(slot < REPS)
            def _():
                give_far(slot, piece).start()

    def poll(chains, step, only):
        def one(piece, carry):
            for take in chains:
                take(step, piece)
            return carry

        if only is None:
            lax.fori_loop(0, PIECES, one, 0)
        else:
            one(only, 0)

    def poll_far(piece):
        for slot in range(REPS - 1):

            @pl.when(slot < at)
            def _():
                long_arrived(slot, piece)

    def project(chain, run, place, strip, with_query=False):
        rows = pl.ds(strip * STRIP, STRIP)
        shards = [chain[4 * run + i + core * (3 - 2 * i), rows] for i in range(REPS)]
        squares = jnp.zeros((STRIP, LANES), f32)
        for shard in shards:
            wide = shard.astype(f32)
            squares += wide * wide
        mean = jnp.sum(squares, axis=1, keepdims=True) * (1.0 / (REPS * LANES))
        whole = jnp.concatenate(shards, axis=1)
        parts = [wbuf[1], wbuf[2]] + ([wbuf[0]] if with_query else [])
        weights = jnp.concatenate(parts, axis=1)
        product = jnp.dot(whole, weights, preferred_element_type=f32)
        product = product * lax.rsqrt(mean + 1e-06)
        count = STRIP // BLOCK
        blocks = pl.ds(strip * count, count)
        for which in range(2):
            piece = product[:, which * LANES : (which + 1) * LANES]
            kv[place, which, blocks] = piece.astype(bf16).reshape(count, BLOCK, LANES)
        if with_query:
            piece = product[:, 2 * LANES :] * HEAD_DIM ** (-0.5)
            qbuf[blocks] = piece.astype(bf16).reshape(count, BLOCK, LANES)

    def kv_copy(index):
        place = 3 - sign * index
        there = place - sign
        return remote(
            kv.at[place], kv.at[there], ksend_sem.at[index], krecv_sem.at[index], sibling
        )

    def wo_rows(column):
        return column, pl.ds(core * (LANES // 2), LANES // 2)

    def wo_copy(turn):
        where = wo_rows(lax.rem(rep + turn, REPS))
        return remote(
            wobuf.at[where],
            owobuf.at[where],
            wo_sem.at[0, turn - 1],
            wo_sem.at[1, turn - 1],
            mate,
        )

    def wo_share(turn):
        where = wo_rows(lax.rem(mate_rep + turn, REPS))
        return remote(
            owobuf.at[where],
            owobuf.at[where],
            wo_sem.at[2, turn - 1],
            wo_sem.at[3, turn - 1],
            sibling,
        )

    def share_weights():
        @pl.when(inner == 1)
        def _():
            for turn in range(1, REPS):
                wo_copy(turn).wait_recv()
                wo_share(turn).start()

    def ready():
        for load in loads:
            load.wait()

        @pl.when(inner == 0)
        def _():
            for turn in range(1, REPS):
                wo_copy(turn).start()

        for there in range(1, REPS):

            def one(piece, carry):
                @pl.when(there > at)
                def _():
                    rows = piece_rows(piece)
                    remote(
                        xlong.at[0, rows],
                        xshort.at[8 + there, rows],
                        give_sem.at[0],
                        take_sem.at[there, piece],
                        sibling,
                    ).wait_recv()

                return carry

            lax.fori_loop(0, PIECES, one, 0)

    chains = {"L": [take_long], "S": [take_short], "B": [take_long, take_short]}
    work = {
        "own": (xshort, 2, 3, 0),
        "long": (xlong, 1, 3 - sign, 1),
        "short": (xshort, 1, 3 - 2 * sign, 2),
        "far": (xlong, 0, 3 - 3 * sign, None),
    }
    for kind, number, piece in SCHEDULE:
        if kind in chains:
            poll(chains[kind], number, piece)
        elif kind == "F":
            poll_far(piece)
        elif kind == "ready":
            ready()
        elif kind == "share":
            share_weights()
        else:
            chain, run, place, index = work[kind]
            project(chain, run, place, number, kind == "own")
            if number == STRIPS - 1 and index is not None:
                kv_copy(index).start()

    for index in range(3):
        kv_copy(index).wait_recv()

    def attend(index):
        query = qbuf[index]
        lane = lax.broadcasted_iota(jnp.int32, (BLOCK, LANES), 1)
        left = lane < HEAD_DIM
        zero = jnp.zeros_like(query)
        both = jnp.concatenate(
            [jnp.where(left, query, zero), jnp.where(left, zero, query)], axis=0
        )
        used = used_ref[index]
        keys, values, counts = [], [], []
        for slot in range(KSLOTS):
            key = key_ref[index, slot]
            place = lax.rem(lax.div(key, BLK_DEV) - blk + 3 + n_blk, n_blk) & 7
            inside = lax.rem(key, BLK_DEV)
            keys.append(kv[place, 0, inside])
            values.append(kv[place, 1, inside])
            counts.append(jnp.where(slot < used, node_ref[key], 0))
        row_lane = lax.broadcasted_iota(jnp.int32, (1, LANES), 1)
        bias = []
        for pair in range(KSLOTS // 2):
            limit = jnp.where(row_lane < BLOCK, counts[2 * pair], counts[2 * pair + 1] + BLOCK)
            bias.append(jnp.where(row_lane < limit, 0.0, NEG))
        bias = jnp.concatenate(bias, axis=1)
        scores = lax.dot_general(
            both,
            jnp.concatenate(keys, axis=0),
            (((1,), (1,)), ((), ())),
            preferred_element_type=jnp.float32,
        )
        scores = scores + bias
        top = jnp.max(scores, axis=1, keepdims=True)
        expo = jnp.exp(scores - top)
        total = jnp.sum(expo, axis=1, keepdims=True)
        mixed = jnp.dot(
            expo.astype(jnp.bfloat16),
            jnp.concatenate(values, axis=0),
            preferred_element_type=jnp.float32,
        )
        mixed = mixed / total
        att[pl.ds(index * BLOCK, BLOCK), :] = jnp.where(
            left, mixed[:BLOCK], mixed[BLOCK:]
        ).astype(jnp.bfloat16)

    def part_rows(part):
        count = PART_ENDS[part] - PART_STARTS[part]
        return pl.ds(PART_STARTS[part] * BLOCK, count * BLOCK)

    def att_copy(part):
        rows = part_rows(part)
        return remote(att.at[rows], oatt.at[rows], att_sem.at[0, part], att_sem.at[1, part], mate)

    def u_copy(part):
        rows = part_rows(part)
        return remote(usend.at[rows], urecv.at[rows], u_sem.at[0, part], u_sem.at[1, part], mate)

    def far_copy(part):
        rows = part_rows(part)
        return remote(
            tsend.at[0, rows], frecv.at[rows], f_sem.at[0, part], f_sem.at[1, part], far
        )

    def peer_copy(part):
        rows = part_rows(part)
        return remote(
            tsend.at[1, rows], trecv.at[rows], t_sem.at[0, part], t_sem.at[1, part], peer
        )

    def two_rows(part):
        rows = part_rows(part)
        return jnp.concatenate([att[rows, :], oatt[rows, :]], axis=1)

    def two_weights(column):
        return jnp.concatenate([wobuf[column], owobuf[column]], axis=0)

    def send_terms(part):
        att_copy(part).wait_recv()
        held = two_rows(part)
        columns = jnp.concatenate([two_weights(far_rep), two_weights(peer_rep)], axis=1)
        terms = jnp.dot(held, columns, preferred_element_type=f32).astype(bf16)
        for which, copy in ((0, far_copy), (1, peer_copy)):
            tsend[which, part_rows(part), :] = terms[:, which * LANES : (which + 1) * LANES]
            copy(part).start()

    @pl.when(inner == 1)
    def _():
        for turn in range(1, REPS):
            wo_share(turn).wait_recv()

    for part in range(PARTS):
        for index in range(PART_STARTS[part], PART_ENDS[part]):
            attend(index)

        @pl.when(inner == 0)
        def _():
            att_copy(part).start()

        @pl.when(inner == 1)
        def _():
            rows = part_rows(part)
            term = jnp.dot(att[rows, :], wobuf[mate_rep], preferred_element_type=f32)
            usend[rows, :] = term.astype(bf16)
            u_copy(part).start()

    def sent(sem):
        remote(xshort.at[0], xshort.at[0], sem, take_sem.at[0, 0], sibling).wait_send()

    def drain():
        sent(cross_sem.at[0])
        for step in range(1, LONG_STEPS):
            sent(lsend_sem.at[8 + at - step])
        for step in range(SHORT_STEPS):
            sent(ssend_sem.at[8 + at - step])
        for step in range(1, REPS):

            @pl.when(at >= step)
            def _():
                sent(give_sem.at[step - 1])

            @pl.when(at < step)
            def _():
                sent(far_give_sem.at[step])

    def settle():
        for index in range(3):
            kv_copy(index).wait_send()
        drain()

    def residual(part):
        return xshort[8 + at, part_rows(part), :].astype(f32)

    @pl.when(inner == 1)
    def _():
        for part in range(PARTS):
            send_terms(part)
        settle()

        for part in range(PARTS):
            rows = part_rows(part)
            mine = jnp.dot(two_rows(part), two_weights(rep), preferred_element_type=f32)
            mine = mine + residual(part)
            peer_copy(part).wait_recv()
            out_ref[rows, :] = (mine + trecv[rows, :].astype(f32)).astype(bf16)
        for part in range(PARTS):
            u_copy(part).wait_send()
            far_copy(part).wait_send()
            peer_copy(part).wait_send()
        for turn in range(1, REPS):
            wo_share(turn).wait_send()

    @pl.when(inner == 0)
    def _():
        settle()

        for part in range(PARTS):
            rows = part_rows(part)
            mine = jnp.dot(att[rows, :], wobuf[rep], preferred_element_type=f32)
            mine = mine + residual(part)
            u_copy(part).wait_recv()
            mine = mine + urecv[rows, :].astype(f32)
            far_copy(part).wait_recv()
            out_ref[rows, :] = (mine + frecv[rows, :].astype(f32)).astype(bf16)
        for part in range(PARTS):
            att_copy(part).wait_send()
        for turn in range(1, REPS):
            wo_copy(turn).wait_send()


def body(x_nodes, w_qkv, w_out, pair_key, pair_count, node_count):
    n_blk = lax.axis_size("blk")
    weights = jnp.transpose(w_qkv, (1, 0, 2))
    vmem = pltpu.VMEM
    dma = pltpu.SemaphoreType.DMA
    return pl.pallas_call(
        functools.partial(kernel, n_blk),
        out_shape=pltpu.VMEM((ROWS, LANES), bf16),
        in_specs=[pl.BlockSpec(memory_space=pltpu.HBM)] * 6,
        out_specs=pl.BlockSpec(memory_space=pltpu.VMEM),
        scratch_shapes=[
            vmem((SLOTS, ROWS, LANES), bf16),
            vmem((SLOTS, ROWS, LANES), bf16),
            vmem((8, 2, BLK_DEV, BLOCK, LANES), bf16),
            vmem((BLK_DEV, BLOCK, LANES), bf16),
            vmem((3, REPS * LANES, LANES), bf16),
            vmem((REPS, LANES, LANES), bf16),
            vmem((REPS, LANES, LANES), bf16),
            vmem((ROWS, LANES), bf16),
            vmem((ROWS, LANES), bf16),
            vmem((2, ROWS, LANES), bf16),
            vmem((ROWS, LANES), bf16),
            vmem((ROWS, LANES), bf16),
            vmem((ROWS, LANES), bf16),
            vmem((ROWS, LANES), bf16),
            pltpu.SMEM(pair_key.shape, jnp.int32),
            pltpu.SMEM(pair_count.shape, jnp.int32),
            pltpu.SMEM(node_count.shape, jnp.int32),
            dma((5 + REPS,)),
            dma((1,)),
            dma((SLOTS,)),
            dma((SLOTS,)),
            dma((SLOTS, PIECES)),
            dma((SLOTS, PIECES)),
            dma((3,)),
            dma((REPS,)),
            dma((REPS, PIECES)),
            dma((3,)),
            dma((3,)),
            dma((4, REPS - 1)),
            dma((2, PARTS)),
            dma((2, PARTS)),
            dma((2, PARTS)),
            dma((2, PARTS)),
        ],
        compiler_params=pltpu.CompilerParams(
            collective_id=0, has_side_effects=True, vmem_limit_bytes=60 << 20
        ),
        name="graph_layer",
    )(x_nodes, weights, w_out, pair_key, pair_count, node_count)


def solution(mesh):
    return jax.shard_map(
        body,
        mesh=mesh,
        in_specs=(
            P("blk", "rep"),
            P(None, None, "rep"),
            P("rep", None),
            P("blk", None),
            P("blk"),
            P(),
        ),
        out_specs=P("blk", "rep"),
        check_vma=False,
    )
```

```python
import functools

import jax
import jax.numpy as jnp
from jax import lax
from jax.experimental import pallas as pl
from jax.experimental.pallas import tpu as pltpu
from jax.sharding import PartitionSpec as P

HEAD_DIM = 64
BLOCK = 64
KSLOTS = 8
LANES = 128
REPS = 4
ROWS = 512
BLK_DEV = 8
SLOTS = 12
LONG_STEPS = 8
SHORT_STEPS = 7
PIECES = 4
PIECE_ROWS = ROWS // PIECES
PART_ENDS = [2, 5, 8]
PARTS = len(PART_ENDS)
PART_STARTS = [0] + PART_ENDS[:-1]
STRIP = 128
STRIPS = ROWS // STRIP
ORDER = [
    "B1", "B2", "B3", "B4", "ready", "B5.0", "own0", "B5.1", "own1", "B5.2", "own2", "B5.3",
    "own3", "B6", "share", "B7.0", "long0", "short0", "B7.1", "long1", "short1", "B7.2",
    "long2", "short2", "B7.3", "long3", "short3", "L8.0", "F.0", "far0", "L8.1", "F.1", "far1",
    "L8.2", "F.2", "far2", "L8.3", "F.3", "far3",
]


def parsed(words):
    found = []
    for word in words:
        kind = word.rstrip("0123456789.")
        number, _, piece = word[len(kind) :].partition(".")
        found.append((kind, int(number or 0), int(piece) if piece else None))
    return found


SCHEDULE = parsed(ORDER)
NEG = -1e30
MESH = pl.DeviceIdType.MESH
bf16 = jnp.bfloat16
f32 = jnp.float32


def kernel(
    n_blk,
    x_ref,
    w_ref,
    wo_ref,
    key_hbm,
    used_hbm,
    node_hbm,
    out_ref,
    xlong,
    xshort,
    kv,
    qbuf,
    wbuf,
    wobuf,
    owobuf,
    att,
    oatt,
    tsend,
    trecv,
    usend,
    urecv,
    frecv,
    key_ref,
    used_ref,
    node_ref,
    local_sem,
    cross_sem,
    lsend_sem,
    ssend_sem,
    lrecv_sem,
    srecv_sem,
    give_sem,
    far_give_sem,
    take_sem,
    ksend_sem,
    krecv_sem,
    wo_sem,
    att_sem,
    t_sem,
    f_sem,
    u_sem,
):
    blk = lax.axis_index("blk")
    rep = lax.axis_index("rep")
    core = lax.rem(blk, 2)
    at = rep + core * (3 - 2 * rep)
    at_end = lax.div(at, 3)
    at_start = lax.div(3 - at, 3)
    sign = 1 - 2 * core
    down_blk = lax.rem(blk + n_blk + 2 * sign * at_end, n_blk)
    up_blk = lax.rem(blk + n_blk - 2 * sign * at_start, n_blk)
    down_rep = lax.rem(rep + REPS + sign, REPS)
    up_rep = lax.rem(rep + REPS - sign, REPS)
    down = (down_blk, down_rep)
    up = (up_blk, up_rep)
    cross = (up_blk + sign, up_rep)
    sibling = (blk + sign, rep)
    inner = lax.rem(lax.div(rep + 1, 2), 2)
    mate_rep = rep + 1 - 2 * lax.rem(rep, 2)
    peer_rep = 3 - rep
    far_rep = lax.rem(rep + 2, REPS)
    drop_blk = lax.rem(blk + 6 * n_blk - 6 * sign * (at_end - at_start), n_blk)
    ends = at_end + at_start
    mate = (blk, mate_rep)
    peer = (blk, peer_rep)
    far = (blk, far_rep)

    barrier = pltpu.get_barrier_semaphore()
    for other in (down, up, cross, sibling, far):
        pl.semaphore_signal(barrier, inc=1, device_id=other, device_id_type=MESH)

    @pl.when(ends == 1)
    def _():
        pl.semaphore_signal(
            barrier,
            inc=1,
            device_id=(drop_blk, at_end * down_rep + at_start * up_rep),
            device_id_type=MESH,
        )

    loads = [
        pltpu.make_async_copy(x_ref, xshort.at[8 + at], local_sem.at[0]),
        pltpu.make_async_copy(w_ref, wbuf, local_sem.at[1]),
        pltpu.make_async_copy(key_hbm, key_ref, local_sem.at[2]),
        pltpu.make_async_copy(used_hbm, used_ref, local_sem.at[3]),
        pltpu.make_async_copy(node_hbm, node_ref, local_sem.at[4]),
    ] + [
        pltpu.make_async_copy(
            wo_ref.at[:, pl.ds(LANES * d, LANES)], wobuf.at[d], local_sem.at[5 + d]
        )
        for d in range(REPS)
    ]
    for load in loads:
        load.start()
    pl.semaphore_wait(barrier, 5 + ends)

    def remote(source, target, send_sem, recv_sem, device):
        return pltpu.make_async_remote_copy(
            src_ref=source,
            dst_ref=target,
            send_sem=send_sem,
            recv_sem=recv_sem,
            device_id=device,
            device_id_type=MESH,
        )

    def piece_rows(piece):
        return pl.ds(piece * PIECE_ROWS, PIECE_ROWS)

    def cross_copy(piece):
        slot = 11 - at - 4 * at_start
        rows = piece_rows(piece)
        return remote(
            x_ref.at[rows],
            xlong.at[slot, rows],
            cross_sem.at[0],
            lrecv_sem.at[slot, piece],
            cross,
        )

    def long_copy(slot, piece):
        rows = piece_rows(piece)
        there = slot - 4 * at_end
        return remote(
            xlong.at[slot, rows],
            xlong.at[there, rows],
            lsend_sem.at[slot],
            lrecv_sem.at[there, piece],
            down,
        )

    def short_copy(slot, piece, source=None):
        rows = piece_rows(piece)
        there = slot - 4 * at_end
        drops = at_end * (1 - lax.div(slot, 8))
        return remote(
            xshort.at[slot, rows] if source is None else source.at[rows],
            xshort.at[there, rows],
            ssend_sem.at[slot],
            srecv_sem.at[there, piece],
            (down_blk + drops * (drop_blk - down_blk), down_rep),
        )

    def give_copy(step, piece):
        rows = piece_rows(piece)
        there = 3 - at + step
        return remote(
            xlong.at[8 + at - step, rows],
            xshort.at[8 + there, rows],
            give_sem.at[step - 1],
            take_sem.at[there],
            sibling,
        )

    def give_far(slot, piece):
        rows = piece_rows(piece)
        return remote(
            xshort.at[slot, rows],
            xlong.at[3 - slot, rows],
            far_give_sem.at[slot],
            lrecv_sem.at[3 - slot, piece],
            sibling,
        )

    for piece in range(PIECES):
        cross_copy(piece).start()
        short_copy(8 + at, piece, x_ref).start()

    def long_arrived(slot, piece):
        rows = piece_rows(piece)
        remote(
            xlong.at[slot, rows],
            xlong.at[slot, rows],
            lsend_sem.at[slot],
            lrecv_sem.at[slot, piece],
            down,
        ).wait_recv()

    def take_long(step, piece):
        slot = 8 + at - step
        long_arrived(slot, piece)
        if step < LONG_STEPS:
            long_copy(slot, piece).start()
        if step < REPS:

            @pl.when(at >= step)
            def _():
                give_copy(step, piece).start()

    def take_short(step, piece):
        slot = 8 + at - step
        rows = piece_rows(piece)
        remote(
            xshort.at[slot, rows],
            xshort.at[slot, rows],
            ssend_sem.at[slot],
            srecv_sem.at[slot, piece],
            down,
        ).wait_recv()
        if step < SHORT_STEPS:
            short_copy(slot, piece).start()
        if step > REPS:

            @pl.when(slot < REPS)
            def _():
                give_far(slot, piece).start()

    def poll(chains, step, only):
        def one(piece, carry):
            for take in chains:
                take(step, piece)
            return carry

        if only is None:
            lax.fori_loop(0, PIECES, one, 0)
        else:
            one(only, 0)

    def poll_far(piece):
        for slot in range(REPS - 1):

            @pl.when(slot < at)
            def _():
                long_arrived(slot, piece)

    def project(chain, run, place, strip, with_query=False):
        rows = pl.ds(strip * STRIP, STRIP)
        shards = [chain[4 * run + i + core * (3 - 2 * i), rows] for i in range(REPS)]
        squares = jnp.zeros((STRIP, LANES), f32)
        for shard in shards:
            wide = shard.astype(f32)
            squares += wide * wide
        mean = jnp.sum(squares, axis=1, keepdims=True) * (1.0 / (REPS * LANES))
        whole = jnp.concatenate(shards, axis=1)
        parts = [wbuf[1], wbuf[2]] + ([wbuf[0]] if with_query else [])
        weights = jnp.concatenate(parts, axis=1)
        product = jnp.dot(whole, weights, preferred_element_type=f32)
        product = product * lax.rsqrt(mean + 1e-06)
        count = STRIP // BLOCK
        blocks = pl.ds(strip * count, count)
        for which in range(2):
            piece = product[:, which * LANES : (which + 1) * LANES]
            kv[place, which, blocks] = piece.astype(bf16).reshape(count, BLOCK, LANES)
        if with_query:
            piece = product[:, 2 * LANES :] * HEAD_DIM ** (-0.5)
            qbuf[blocks] = piece.astype(bf16).reshape(count, BLOCK, LANES)

    def kv_copy(index):
        place = 3 - sign * index
        there = place - sign
        return remote(
            kv.at[place], kv.at[there], ksend_sem.at[index], krecv_sem.at[index], sibling
        )

    def wo_rows(column):
        return column, pl.ds(core * (LANES // 2), LANES // 2)

    def wo_copy(turn):
        where = wo_rows(lax.rem(rep + turn, REPS))
        return remote(
            wobuf.at[where],
            owobuf.at[where],
            wo_sem.at[0, turn - 1],
            wo_sem.at[1, turn - 1],
            mate,
        )

    def wo_share(turn):
        where = wo_rows(lax.rem(mate_rep + turn, REPS))
        return remote(
            owobuf.at[where],
            owobuf.at[where],
            wo_sem.at[2, turn - 1],
            wo_sem.at[3, turn - 1],
            sibling,
        )

    def share_weights():
        @pl.when(inner == 1)
        def _():
            for turn in range(1, REPS):
                wo_copy(turn).wait_recv()
                wo_share(turn).start()

    def ready():
        for load in loads:
            load.wait()

        @pl.when(inner == 0)
        def _():
            for turn in range(1, REPS):
                wo_copy(turn).start()

        for there in range(1, REPS):

            @pl.when(there > at)
            def _():
                remote(
                    xlong.at[0], xshort.at[8 + there], give_sem.at[0], take_sem.at[there], sibling
                ).wait_recv()

    chains = {"L": [take_long], "S": [take_short], "B": [take_long, take_short]}
    work = {
        "own": (xshort, 2, 3, 0),
        "long": (xlong, 1, 3 - sign, 1),
        "short": (xshort, 1, 3 - 2 * sign, 2),
        "far": (xlong, 0, 3 - 3 * sign, None),
    }
    for kind, number, piece in SCHEDULE:
        if kind in chains:
            poll(chains[kind], number, piece)
        elif kind == "F":
            poll_far(piece)
        elif kind == "ready":
            ready()
        elif kind == "share":
            share_weights()
        else:
            chain, run, place, index = work[kind]
            project(chain, run, place, number, kind == "own")
            if number == STRIPS - 1 and index is not None:
                kv_copy(index).start()

    for index in range(3):
        kv_copy(index).wait_recv()

    def attend(index):
        query = qbuf[index]
        lane = lax.broadcasted_iota(jnp.int32, (BLOCK, LANES), 1)
        left = lane < HEAD_DIM
        zero = jnp.zeros_like(query)
        both = jnp.concatenate(
            [jnp.where(left, query, zero), jnp.where(left, zero, query)], axis=0
        )
        used = used_ref[index]
        keys, values, counts = [], [], []
        for slot in range(KSLOTS):
            key = key_ref[index, slot]
            place = lax.rem(lax.div(key, BLK_DEV) - blk + 3 + n_blk, n_blk) & 7
            inside = lax.rem(key, BLK_DEV)
            keys.append(kv[place, 0, inside])
            values.append(kv[place, 1, inside])
            counts.append(jnp.where(slot < used, node_ref[key], 0))
        row_lane = lax.broadcasted_iota(jnp.int32, (1, LANES), 1)
        bias = []
        for pair in range(KSLOTS // 2):
            limit = jnp.where(row_lane < BLOCK, counts[2 * pair], counts[2 * pair + 1] + BLOCK)
            bias.append(jnp.where(row_lane < limit, 0.0, NEG))
        bias = jnp.concatenate(bias, axis=1)
        scores = lax.dot_general(
            both,
            jnp.concatenate(keys, axis=0),
            (((1,), (1,)), ((), ())),
            preferred_element_type=jnp.float32,
        )
        scores = scores + bias
        top = jnp.max(scores, axis=1, keepdims=True)
        expo = jnp.exp(scores - top)
        total = jnp.sum(expo, axis=1, keepdims=True)
        mixed = jnp.dot(
            expo.astype(jnp.bfloat16),
            jnp.concatenate(values, axis=0),
            preferred_element_type=jnp.float32,
        )
        mixed = mixed / total
        att[pl.ds(index * BLOCK, BLOCK), :] = jnp.where(
            left, mixed[:BLOCK], mixed[BLOCK:]
        ).astype(jnp.bfloat16)

    def part_rows(part):
        count = PART_ENDS[part] - PART_STARTS[part]
        return pl.ds(PART_STARTS[part] * BLOCK, count * BLOCK)

    def att_copy(part):
        rows = part_rows(part)
        return remote(att.at[rows], oatt.at[rows], att_sem.at[0, part], att_sem.at[1, part], mate)

    def u_copy(part):
        rows = part_rows(part)
        return remote(usend.at[rows], urecv.at[rows], u_sem.at[0, part], u_sem.at[1, part], mate)

    def far_copy(part):
        rows = part_rows(part)
        return remote(
            tsend.at[0, rows], frecv.at[rows], f_sem.at[0, part], f_sem.at[1, part], far
        )

    def peer_copy(part):
        rows = part_rows(part)
        return remote(
            tsend.at[1, rows], trecv.at[rows], t_sem.at[0, part], t_sem.at[1, part], peer
        )

    def two_rows(part):
        rows = part_rows(part)
        return jnp.concatenate([att[rows, :], oatt[rows, :]], axis=1)

    def two_weights(column):
        return jnp.concatenate([wobuf[column], owobuf[column]], axis=0)

    def send_terms(part):
        att_copy(part).wait_recv()
        held = two_rows(part)
        columns = jnp.concatenate([two_weights(far_rep), two_weights(peer_rep)], axis=1)
        terms = jnp.dot(held, columns, preferred_element_type=f32).astype(bf16)
        for which, copy in ((0, far_copy), (1, peer_copy)):
            tsend[which, part_rows(part), :] = terms[:, which * LANES : (which + 1) * LANES]
            copy(part).start()

    @pl.when(inner == 1)
    def _():
        for turn in range(1, REPS):
            wo_share(turn).wait_recv()

    for part in range(PARTS):
        for index in range(PART_STARTS[part], PART_ENDS[part]):
            attend(index)

        @pl.when(inner == 0)
        def _():
            att_copy(part).start()

        @pl.when(inner == 1)
        def _():
            rows = part_rows(part)
            term = jnp.dot(att[rows, :], wobuf[mate_rep], preferred_element_type=f32)
            usend[rows, :] = term.astype(bf16)
            u_copy(part).start()

    def sent(sem):
        remote(xshort.at[0], xshort.at[0], sem, take_sem.at[0], sibling).wait_send()

    def drain():
        sent(cross_sem.at[0])
        for step in range(1, LONG_STEPS):
            sent(lsend_sem.at[8 + at - step])
        for step in range(SHORT_STEPS):
            sent(ssend_sem.at[8 + at - step])
        for step in range(1, REPS):

            @pl.when(at >= step)
            def _():
                sent(give_sem.at[step - 1])

            @pl.when(at < step)
            def _():
                sent(far_give_sem.at[step])

    def settle():
        for index in range(3):
            kv_copy(index).wait_send()
        drain()

    def residual(part):
        return xshort[8 + at, part_rows(part), :].astype(f32)

    @pl.when(inner == 1)
    def _():
        for part in range(PARTS):
            send_terms(part)
        settle()
        for turn in range(1, REPS):
            wo_share(turn).wait_send()
        for part in range(PARTS):
            u_copy(part).wait_send()

        for part in range(PARTS):
            rows = part_rows(part)
            mine = jnp.dot(two_rows(part), two_weights(rep), preferred_element_type=f32)
            mine = mine + residual(part)
            peer_copy(part).wait_recv()
            out_ref[rows, :] = (mine + trecv[rows, :].astype(f32)).astype(bf16)
        for part in range(PARTS):
            far_copy(part).wait_send()
            peer_copy(part).wait_send()

    @pl.when(inner == 0)
    def _():
        settle()
        for turn in range(1, REPS):
            wo_copy(turn).wait_send()
        for part in range(PARTS):
            att_copy(part).wait_send()

        for part in range(PARTS):
            rows = part_rows(part)
            mine = jnp.dot(att[rows, :], wobuf[rep], preferred_element_type=f32)
            mine = mine + residual(part)
            u_copy(part).wait_recv()
            mine = mine + urecv[rows, :].astype(f32)
            far_copy(part).wait_recv()
            out_ref[rows, :] = (mine + frecv[rows, :].astype(f32)).astype(bf16)


def body(x_nodes, w_qkv, w_out, pair_key, pair_count, node_count):
    n_blk = lax.axis_size("blk")
    weights = jnp.transpose(w_qkv, (1, 0, 2))
    vmem = pltpu.VMEM
    dma = pltpu.SemaphoreType.DMA
    return pl.pallas_call(
        functools.partial(kernel, n_blk),
        out_shape=pltpu.VMEM((ROWS, LANES), bf16),
        in_specs=[pl.BlockSpec(memory_space=pltpu.HBM)] * 6,
        out_specs=pl.BlockSpec(memory_space=pltpu.VMEM),
        scratch_shapes=[
            vmem((SLOTS, ROWS, LANES), bf16),
            vmem((SLOTS, ROWS, LANES), bf16),
            vmem((8, 2, BLK_DEV, BLOCK, LANES), bf16),
            vmem((BLK_DEV, BLOCK, LANES), bf16),
            vmem((3, REPS * LANES, LANES), bf16),
            vmem((REPS, LANES, LANES), bf16),
            vmem((REPS, LANES, LANES), bf16),
            vmem((ROWS, LANES), bf16),
            vmem((ROWS, LANES), bf16),
            vmem((2, ROWS, LANES), bf16),
            vmem((ROWS, LANES), bf16),
            vmem((ROWS, LANES), bf16),
            vmem((ROWS, LANES), bf16),
            vmem((ROWS, LANES), bf16),
            pltpu.SMEM(pair_key.shape, jnp.int32),
            pltpu.SMEM(pair_count.shape, jnp.int32),
            pltpu.SMEM(node_count.shape, jnp.int32),
            dma((5 + REPS,)),
            dma((1,)),
            dma((SLOTS,)),
            dma((SLOTS,)),
            dma((SLOTS, PIECES)),
            dma((SLOTS, PIECES)),
            dma((3,)),
            dma((REPS,)),
            dma((REPS,)),
            dma((3,)),
            dma((3,)),
            dma((4, REPS - 1)),
            dma((2, PARTS)),
            dma((2, PARTS)),
            dma((2, PARTS)),
            dma((2, PARTS)),
        ],
        compiler_params=pltpu.CompilerParams(
            collective_id=0, has_side_effects=True, vmem_limit_bytes=60 << 20
        ),
        name="graph_layer",
    )(x_nodes, weights, w_out, pair_key, pair_count, node_count)


def solution(mesh):
    return jax.shard_map(
        body,
        mesh=mesh,
        in_specs=(
            P("blk", "rep"),
            P(None, None, "rep"),
            P("rep", None),
            P("blk", None),
            P("blk"),
            P(),
        ),
        out_specs=P("blk", "rep"),
        check_vma=False,
    )
```
